128 devices in a mesh: fsdp: 8 (over z, y_hi), cb: 16 (over y_lo, x, core).
Axes of the slice: x: 4, y: 4 (y_hi: 2, y_lo: 2; y = y_hi * 2 + y_lo), z: 4, core: 2. Of those that a mesh axis runs over, the one named last changes fastest.
Arguments:
- frames_in: bfloat16 [8, 256, 6144], P('fsdp', 'cb'), may hold values from -6 to 6
- valid_len: int32 [8], P('fsdp'), may hold values from 128 to 256
- tokens: int32 [8, 16, 256], P('fsdp', 'cb'), may hold values from 0 to 2047
- t_gain: float32 [6144], replicated, may hold values from 0.25 to 1.75
- w_qkv: bfloat16 [6144, 12288], P('fsdp', 'cb'), as said below
- w_out: bfloat16 [4096, 6144], P('cb', 'fsdp'), may hold values from -0.09375 to 0.09375
- h_gain: float32 [6144], replicated, may hold values from 0.25 to 1.75
- d_in: bfloat16 [16, 6144, 1024], P('cb'), may hold values from -0.078125 to 0.078125
- d_embed: bfloat16 [16, 2048, 1024], P('cb'), may hold values from -6 to 6
- d_gain: float32 [16, 1024], P('cb'), may hold values from 0.25 to 1.75
- d_qkv: bfloat16 [16, 1024, 3072], P('cb'), as said below
Outputs:
- depth_mix: bfloat16 [8, 16, 256, 1024], P('fsdp', 'cb')
The draws below stay inside these ranges and needn't reach their ends.
Inputs may be any that keep to these rules, and one draw needn't show every extreme that they name: `w_qkv`: every entry of the temporal projections has magnitude at most 31 / sqrt(6144). `d_qkv`: every entry of the depth projections has magnitude at most 31 / sqrt(1024).
All inputs are finite; a program needn't handle non-finite values.
Results may differ from the reference program's by a relative error of at most 0.012.
Values may be sent and summed in bfloat16 or wider, within the bound.
No kernel may reach another device: no remote copies, remote signals or barrier semaphores. Data moves between devices by JAX's collectives and lax.ppermute only.
A program may use at most 128 MiB of HBM per device.

```python
import math
import jax
import jax.numpy as jnp
import numpy as np
from jax import lax

D = 6144
HEADS = 32
HEAD = 128
LENGTH = 256
DD = 1024
DHEADS = 16
DHEAD = 64
CARD = 2048
SEQS = 8
CODEBOOKS = 16


def draw_w_qkv(key, part):
    first = jax.random.fold_in(jax.random.fold_in(key, 11), 0)
    parts = jnp.clip(jax.random.normal(first, (D, HEADS, 3, HEAD), jnp.float32), -4.0, 4.0)
    return (parts * D ** (-0.5)).reshape(D, 3 * HEADS * HEAD).astype(jnp.bfloat16)


def draw_d_qkv(key, part):
    first = jax.random.fold_in(jax.random.fold_in(key, 23), 0)
    parts = jnp.clip(jax.random.normal(first, (CODEBOOKS, DD, 3, DHEADS, DHEAD), jnp.float32), -4.0, 4.0)
    return (parts * DD ** (-0.5)).reshape(CODEBOOKS, DD, 3 * DD).astype(jnp.bfloat16)


def touch_ends(array, rng, smallest, largest):
    longest = array.shape.index(max(array.shape))
    spots = []
    for shift in (0, 1):
        where = [jax.random.randint(jax.random.fold_in(rng, axis), (), 0, length) for axis, length in enumerate(array.shape)]
        where[longest] = (where[longest] + shift) % array.shape[longest]
        spots.append(tuple(where))
    return array.at[spots[0]].set(smallest).at[spots[1]].set(largest)


def block_scale(rng, extent, cuts, low, high):
    def one(position, blocks):
        steps = jax.random.uniform(jax.random.fold_in(jax.random.fold_in(rng, 6), position), (blocks,), jnp.float32, low / len(cuts), high / len(cuts))
        return jnp.repeat(jnp.exp(steps), extent[position] // blocks).reshape((-1,) + (1,) * (len(extent) - position - 1))

    level = one(*cuts[0])
    for cut in cuts[1:]:
        level = level * one(*cut)
    return level


def rank_table(number_of, lean):
    weights = [(1 << 20) // math.isqrt(standing ** lean) + 1 for standing in range(1, number_of + 1)]
    width = 1 + sum(weights) // (1 << 30)
    return np.cumsum(np.array([max(1, weight // width) for weight in weights]))


def skewed_ids(stream_key, dims, amount, lean):
    grid = rank_table(amount, lean)
    pick = jax.random.randint(jax.random.fold_in(stream_key, 1), dims, 0, int(grid[amount - 1]))
    grade = jnp.searchsorted(jnp.asarray(grid, jnp.int32), pick, side="right")
    return jax.random.permutation(jax.random.fold_in(stream_key, 2), amount)[grade].astype(jnp.int32)


def scatter_about(own_key, shape, deviation, limit, cuts=(), held_as=jnp.bfloat16):
    values = jax.random.normal(own_key, shape, jnp.float32) * deviation
    if len(cuts) > 0:
        values = block_scale(own_key, shape, cuts, -0.22, 0.18) * values
    return jnp.clip(values, min=-limit, max=limit).astype(held_as)


def setup_inputs(seed: int = 0) -> dict:
    streams_of = jax.random.split(jax.random.key(seed), 12)
    return {
        "frames_in": scatter_about(streams_of[0], (SEQS, LENGTH, D), 1.0, 6.0, ((0, 8), (1, 16))),
        "valid_len": touch_ends(jax.random.randint(streams_of[1], (SEQS,), LENGTH // 2, LENGTH + 1), jax.random.fold_in(streams_of[1], 1), LENGTH // 2, LENGTH).astype(jnp.int32),
        "tokens": touch_ends(skewed_ids(streams_of[2], (SEQS, CODEBOOKS, LENGTH), CARD, 2), jax.random.fold_in(streams_of[2], 3), 0, CARD - 1).astype(jnp.int32),
        "t_gain": jnp.clip(1.0 + 0.15 * jax.random.normal(streams_of[3], (D,), jnp.float32), 0.25, 1.75),
        "w_qkv": draw_w_qkv(jax.random.fold_in(streams_of[11], 71), 0),
        "w_out": scatter_about(streams_of[5], (HEADS * HEAD, D), (HEADS * HEAD) ** -0.5, 0.09375, ((0, 16), (1, 8))),
        "h_gain": jnp.clip(1.0 + 0.15 * jax.random.normal(streams_of[6], (D,), jnp.float32), 0.25, 1.75),
        "d_in": scatter_about(streams_of[7], (CODEBOOKS, D, DD), D ** -0.5, 0.078125, ((0, 16),)),
        "d_embed": scatter_about(streams_of[8], (CODEBOOKS, CARD, DD), 1.0, 6.0, ((0, 16),)),
        "d_gain": jnp.clip(1.0 + 0.15 * jax.random.normal(streams_of[9], (CODEBOOKS, DD), jnp.float32), 0.25, 1.75),
        "d_qkv": draw_d_qkv(jax.random.fold_in(streams_of[11], 71), 0),
    }


EPS = 1e-05
NEG = -1e+30

def rms_scale(values, gain):
    mean_sq = lax.optimization_barrier(jnp.mean(values * values, axis=-1, keepdims=True))
    return values * lax.rsqrt(mean_sq + EPS) * gain

def reference(frames_in, valid_len, tokens, t_gain, w_qkv, w_out, h_gain, d_in, d_embed, d_gain, d_qkv):
    base = frames_in.astype(jnp.float32)
    normed = rms_scale(base, t_gain).astype(jnp.bfloat16)
    packed = jnp.dot(normed.reshape(SEQS * LENGTH, D), w_qkv, preferred_element_type=jnp.float32).astype(jnp.bfloat16)
    packed = packed.reshape(SEQS, LENGTH, HEADS, 3, HEAD).astype(jnp.float32)
    query = packed[:, :, :, 0]
    keys = packed[:, :, :, 1]
    values = packed[:, :, :, 2]
    scores = jnp.einsum('sihe,sjhe->shij', query, keys) / math.sqrt(HEAD)
    rows = jnp.arange(LENGTH, dtype=jnp.int32)[:, None]
    cols = jnp.arange(LENGTH, dtype=jnp.int32)[None, :]
    allowed = (cols <= rows)[None, None] & (cols[None, None] < valid_len[:, None, None, None])
    scores = jnp.where(allowed, scores, NEG)
    top = lax.optimization_barrier(jnp.max(scores, axis=-1, keepdims=True))
    expo = jnp.where(allowed, jnp.exp(scores - top), 0.0)
    probs = (expo / lax.optimization_barrier(jnp.sum(expo, axis=-1, keepdims=True))).astype(jnp.bfloat16)
    mixed = jnp.einsum('shij,sjhe->sihe', probs.astype(jnp.float32), values).astype(jnp.bfloat16)
    proj = jnp.dot(mixed.reshape(SEQS * LENGTH, HEADS * HEAD), w_out, preferred_element_type=jnp.float32)
    hidden = base + proj.reshape(SEQS, LENGTH, D)
    hnorm = rms_scale(hidden, h_gain).astype(jnp.bfloat16).reshape(SEQS * LENGTH, D)

    def section(inputs):
        weight_in, table, gain, weight_qkv, ids = inputs
        lifted = jnp.dot(hnorm, weight_in, preferred_element_type=jnp.float32).reshape(SEQS, LENGTH, DD)
        lifted = lifted + jnp.take(table, ids, axis=0).astype(jnp.float32)
        dnorm = rms_scale(lifted, gain).astype(jnp.bfloat16)
        result = jnp.dot(dnorm.reshape(SEQS * LENGTH, DD), weight_qkv, preferred_element_type=jnp.float32)
        return result.astype(jnp.bfloat16).reshape(SEQS, LENGTH, 3 * DD)
    dqkv = lax.map(section, (d_in, d_embed, d_gain, d_qkv, jnp.swapaxes(tokens, 0, 1)))
    dq = dqkv[..., :DD].reshape(CODEBOOKS, SEQS, LENGTH, DHEADS, DHEAD).astype(jnp.float32)
    dk = dqkv[..., DD:2 * DD].reshape(CODEBOOKS, SEQS, LENGTH, DHEADS, DHEAD).astype(jnp.float32)
    dv = dqkv[..., 2 * DD:].reshape(CODEBOOKS, SEQS, LENGTH, DHEADS, DHEAD).astype(jnp.float32)
    dscore = jnp.einsum('csihe,jsihe->sihcj', dq, dk) / math.sqrt(DHEAD)
    causal = jnp.arange(CODEBOOKS, dtype=jnp.int32)[:, None] >= jnp.arange(CODEBOOKS, dtype=jnp.int32)[None, :]
    dscore = jnp.where(causal, dscore, NEG)
    dtop = lax.optimization_barrier(jnp.max(dscore, axis=-1, keepdims=True))
    dexp = jnp.where(causal, jnp.exp(dscore - dtop), 0.0)
    dprob = dexp / lax.optimization_barrier(jnp.sum(dexp, axis=-1, keepdims=True))
    out = jnp.einsum('sihcj,jsihe->scihe', dprob, dv)
    return out.reshape(SEQS, CODEBOOKS, LENGTH, DD).astype(jnp.bfloat16)
```

```python
import functools
import math

import jax
import jax.numpy as jnp
from jax import lax
from jax.experimental import pallas as pl
from jax.experimental.pallas import tpu as pltpu
from jax.sharding import PartitionSpec as P

HEAD = 128
DHEAD = 64
EPS = 1e-05
NEG = -1e30
BF = jnp.bfloat16
F32 = jnp.float32


VM = pl.BlockSpec(memory_space=pltpu.VMEM)
SM = pl.BlockSpec(memory_space=pltpu.SMEM)


def swap(value, axis, size, flip):
    return lax.ppermute(value, axis, [(i, i ^ flip) for i in range(size)])


def call(kernel, outs, scratch=(), smem=0, n_in=0):
    return pl.pallas_call(
        kernel,
        out_shape=[jax.ShapeDtypeStruct(s, d) for s, d in outs],
        in_specs=[SM] * smem + [VM] * (n_in - smem),
        out_specs=[VM] * len(outs),
        scratch_shapes=list(scratch),
    )


def norm_kernel(ids, x_ref, g_ref, o_ref):
    x = x_ref[...].astype(F32)
    scale = lax.rsqrt(jnp.mean(x * x, axis=-1, keepdims=True) + EPS)
    y = (x * scale * g_ref[...]).astype(BF)
    width = o_ref.shape[2]
    for b in range(o_ref.shape[0]):
        o_ref[ids[0] ^ b] = y[:, b * width:(b + 1) * width]


def qkv_kernel(g_ref, h_ref, w0_ref, w1_ref, *outs):
    width = w0_ref.shape[0]
    for d, o_ref in enumerate(outs):
        for kk, src in enumerate((g_ref, h_ref)):
            a = src[:, 2 * d].reshape(-1, width)
            b = src[:, 2 * d + 1].reshape(-1, width)
            acc = jnp.dot(a, w0_ref[...], preferred_element_type=F32)
            acc = acc + jnp.dot(b, w1_ref[...], preferred_element_type=F32)
            rows = acc.shape[0]
            o_ref[kk * rows:(kk + 1) * rows, :] = acc.astype(o_ref.dtype)


def place(row, section, step):
    group = row // step
    half = group // 8
    return (section ^ (2 * (group - 8 * half) + half)) * step + (row - group * step)


def attn_kernel(ids, own, r1, r2, r3, *rest):
    wo = rest[:8]
    outs = rest[8:10]
    packed = rest[10]
    mixed = rest[11]
    length = own.shape[0]
    packed[...] = (
        own[...] + r1[...].astype(F32) + r2[...].astype(F32) + r3[...].astype(F32)
    ).astype(BF)
    section = ids[1]
    valid = ids[2]
    rows = place(lax.broadcasted_iota(jnp.int32, (length, 1), 0), section, 16)
    cols = place(lax.broadcasted_iota(jnp.int32, (1, length), 1), section, 16)
    allowed = (cols <= rows) & (cols < valid)
    for h in range(own.shape[1] // (3 * HEAD)):
        base = h * 3 * HEAD
        q = packed[:, base:base + HEAD]
        k = packed[:, base + HEAD:base + 2 * HEAD]
        v = packed[:, base + 2 * HEAD:base + 3 * HEAD]
        s = lax.dot_general(q, k, (((1,), (1,)), ((), ())), preferred_element_type=F32)
        s = jnp.where(allowed, s * (1.0 / math.sqrt(HEAD)), NEG)
        top = jnp.max(s, axis=-1, keepdims=True)
        e = jnp.where(allowed, jnp.exp(s - top), 0.0)
        p = (e / jnp.sum(e, axis=-1, keepdims=True)).astype(BF)
        mixed[:, h * HEAD:(h + 1) * HEAD] = jnp.dot(
            p, v, preferred_element_type=F32
        ).astype(BF)
    half = length // 2
    width = wo[0].shape[1]
    for e in range(8):
        acc = jnp.dot(mixed[...], wo[e][...], preferred_element_type=F32).astype(BF)
        outs[0][:, e * width:(e + 1) * width] = acc[:half]
        outs[1][:, e * width:(e + 1) * width] = acc[half:]


def pair_kernel(a_ref, b_ref, *outs):
    for j, o_ref in enumerate(outs):
        rows = o_ref.shape[0]
        part = a_ref[j * rows:(j + 1) * rows, :].astype(F32) + b_ref[
            j * rows:(j + 1) * rows, :
        ].astype(F32)
        o_ref[...] = part.astype(o_ref.dtype)


def hidden_kernel(ids, frames, gain, *rest):
    pieces = rest[:8]
    o_ref = rest[8]
    acc = rest[9]
    width = frames.shape[1] // 8
    for e in range(8):
        cut = slice(e * width, (e + 1) * width)
        part = pieces[0][:, cut].astype(F32)
        for piece in pieces[1:]:
            part = part + piece[:, cut].astype(F32)
        acc[ids[0] ^ e] = part
    total = jnp.zeros((frames.shape[0], 1), F32)
    for b in range(8):
        cut = slice(b * width, (b + 1) * width)
        hid = frames[:, cut].astype(F32) + acc[b]
        acc[b] = hid
        total = total + jnp.sum(hid * hid, axis=-1, keepdims=True)
    scale = lax.rsqrt(total / frames.shape[1] + EPS)
    for b in range(8):
        cut = slice(b * width, (b + 1) * width)
        o_ref[:, cut] = (acc[b] * scale * gain[:, cut]).astype(BF)


def lift_kernel(g_ref, h_ref, din, emb, gain, wqkv, *outs):
    width = g_ref.shape[2]
    parts = []
    for src in (g_ref, h_ref):
        parts.append(src[...].reshape(-1, width))
    x = jnp.concatenate(parts, axis=0)
    lifted = jnp.dot(x, din[...], preferred_element_type=F32) + emb[...].astype(F32)
    scale = lax.rsqrt(jnp.mean(lifted * lifted, axis=-1, keepdims=True) + EPS)
    dn = (lifted * scale * gain[...]).astype(BF)
    step = 1024
    for s in range(wqkv.shape[1] // step):
        cut = slice(s * step, (s + 1) * step)
        y = jnp.dot(dn, wqkv[:, cut], preferred_element_type=F32).astype(BF)
        for e in range(8):
            outs[e][0, :, cut] = y[e * 16:(e + 1) * 16]
            outs[e][1, :, cut] = y[128 + e * 16:128 + (e + 1) * 16]


def depth_kernel(ids, *rest):
    pieces = rest[:8]
    other = rest[8]
    outs = rest[9:17]
    z = rest[17]
    for e in range(8):
        z[e * 16:(e + 1) * 16, :] = pieces[e][0]
        z[128 + e * 16:128 + (e + 1) * 16, :] = other[e]
    section = ids[1]
    rows = lax.broadcasted_iota(jnp.int32, (256, 1), 0)
    cols = lax.broadcasted_iota(jnp.int32, (1, 256), 1)
    rpos = place(rows, section, 16) // 16
    cpos = place(cols, section, 16) // 16
    keep = (cpos <= rpos) & (rows % 16 == cols % 16)
    bias = jnp.where(keep, 0.0, NEG)
    lane = lax.broadcasted_iota(jnp.int32, (256, 2 * DHEAD), 1)
    low = lane < DHEAD
    inner = z.shape[1] // 3
    for pair in range(inner // (2 * DHEAD)):
        base = pair * 2 * DHEAD
        q = z[:, base:base + 2 * DHEAD]
        k = z[:, inner + base:inner + base + 2 * DHEAD]
        v = z[:, 2 * inner + base:2 * inner + base + 2 * DHEAD]
        got = []
        for side in range(2):
            mask = low if side == 0 else jnp.logical_not(low)
            qs = jnp.where(mask, q, jnp.zeros_like(q))
            s = lax.dot_general(
                qs, k, (((1,), (1,)), ((), ())), preferred_element_type=F32
            )
            s = s * (1.0 / math.sqrt(DHEAD)) + bias
            top = jnp.max(s, axis=-1, keepdims=True)
            e = jnp.exp(s - top)
            total = jnp.sum(e, axis=-1, keepdims=True)
            o = jnp.dot(e.astype(BF), v, preferred_element_type=F32)
            got.append(o / total)
        res = jnp.where(low, got[0], got[1]).astype(BF)
        for e in range(8):
            outs[e][0, :, base:base + 2 * DHEAD] = res[e * 16:(e + 1) * 16]
            outs[e][1, :, base:base + 2 * DHEAD] = res[128 + e * 16:128 + (e + 1) * 16]


def final_kernel(ids, *rest):
    pieces = rest[:8]
    other = rest[8]
    o_ref = rest[9]
    for e in range(8):
        o_ref[ids[1] ^ (2 * e)] = pieces[e][0]
        o_ref[ids[1] ^ (2 * e + 1)] = other[e]


def body(frames_in, valid_len, tokens, t_gain, w_qkv, w_out, h_gain, d_in, d_embed, d_gain, d_qkv):
    model = frames_in.shape[2]
    mine = frames_in[0]
    f = lax.axis_index("fsdp").astype(jnp.int32)
    c = lax.axis_index("cb").astype(jnp.int32)
    ids = jnp.stack([f, c, valid_len[0]])
    fs = lambda v, flip: swap(v, "fsdp", 8, flip)
    cb = lambda v, flip: swap(v, "cb", 16, flip)
    block = model // 8

    rel = call(norm_kernel, [((8, 16, block), BF)], smem=1, n_in=3)(
        ids, mine, t_gain[None]
    )[0]
    w_other = fs(w_qkv, 1)
    wo_other = fs(w_out, 1)
    local = [rel[0:2]] + [fs(rel[2 * d:2 * d + 2], 2 * d) for d in (1, 2, 3)]
    local = jnp.concatenate(local, axis=0)
    got = [local] + [cb(local, 2 * e) for e in range(1, 8)]
    even = jnp.stack(got)
    odd = cb(even, 1)
    cols = w_qkv.shape[1]
    parts = call(
        qkv_kernel, [((256, cols), F32)] + [((256, cols), BF)] * 3, n_in=4
    )(even, odd, w_qkv, w_other)
    wo_pair = jnp.stack([w_out, wo_other])
    wo_far = [fs(wo_pair, 2 * d) for d in (1, 2, 3)]
    wo = [w_out, wo_other]
    for pair in wo_far:
        wo += [pair[0], pair[1]]
    sums = [fs(parts[d], 2 * d) for d in (1, 2, 3)]
    keep, give = call(
        attn_kernel,
        [((128, model), BF)] * 2,
        scratch=[pltpu.VMEM((256, cols), BF), pltpu.VMEM((256, w_out.shape[0]), BF)],
        smem=1,
        n_in=13,
    )(ids, parts[0], *sums, *wo)
    taken = cb(give, 1)
    blocks = call(pair_kernel, [((16, model), F32)] + [((16, model), BF)] * 7, n_in=2)(
        keep, taken
    )
    pieces = [blocks[0]] + [cb(blocks[e], 2 * e) for e in range(1, 8)]
    hn = call(
        hidden_kernel,
        [((16, model), BF)],
        scratch=[pltpu.VMEM((8, 16, block), F32)],
        smem=1,
        n_in=11,
    )(ids, mine, h_gain[None], *pieces)[0]
    even = jnp.stack([hn] + [cb(hn, 2 * e) for e in range(1, 8)])
    odd = cb(even, 1)

    order = jnp.concatenate([2 * jnp.arange(8), 2 * jnp.arange(8) + 1]).astype(jnp.int32)
    ids_rel = jnp.take(tokens[0, 0].reshape(16, 16), c ^ order, axis=0).reshape(256)
    emb = jnp.take(d_embed[0], ids_rel, axis=0)
    inner = d_in.shape[2]
    sent = call(lift_kernel, [((2, 16, 3 * inner), BF)] * 8, n_in=6)(
        even, odd, d_in[0], emb, d_gain, d_qkv[0]
    )
    pieces = [sent[0]] + [cb(sent[e], 2 * e) for e in range(1, 8)]
    other = cb(jnp.stack([p[1] for p in pieces]), 1)
    outs = call(
        depth_kernel,
        [((2, 16, inner), BF)] * 8,
        scratch=[pltpu.VMEM((256, 3 * inner), BF)],
        smem=1,
        n_in=10,
    )(ids, *pieces, other)
    pieces = [outs[0]] + [cb(outs[e], 2 * e) for e in range(1, 8)]
    other = cb(jnp.stack([p[1] for p in pieces]), 1)
    out = call(final_kernel, [((16, 16, inner), BF)], smem=1, n_in=10)(
        ids, *pieces, other
    )[0]
    return out.reshape(1, 1, 256, inner)


def solution(mesh):
    placed = (
        P("fsdp", "cb", None),
        P("fsdp"),
        P("fsdp", "cb", None),
        P(),
        P("fsdp", "cb"),
        P("cb", "fsdp"),
        P(),
        P("cb", None, None),
        P("cb", None, None),
        P("cb", None),
        P("cb", None, None),
    )
    return jax.shard_map(
        body, mesh=mesh, in_specs=placed, out_specs=P("fsdp", "cb", None, None), check_vma=False
    )
```

```python
import math

import jax
import jax.numpy as jnp
from jax import lax
from jax.experimental import pallas as pl
from jax.experimental.pallas import tpu as pltpu
from jax.sharding import PartitionSpec as P


HEAD = 128
DHEAD = 64
EPS = 1e-05
NEG = -1e30
BF = jnp.bfloat16
F32 = jnp.float32


VM = pl.BlockSpec(memory_space=pltpu.VMEM)
SM = pl.BlockSpec(memory_space=pltpu.SMEM)


def swap(value, axis, size, flip):
    return lax.ppermute(value, axis, [(i, i ^ flip) for i in range(size)])


def call(kernel, outs, scratch=(), smem=0, n_in=0, limit=8, last=False):
    kind = jax.ShapeDtypeStruct if last else pltpu.VMEM
    run = pl.pallas_call(
        kernel,
        out_shape=[kind(s, d) for s, d in outs],
        in_specs=[SM] * smem + [VM] * (n_in - smem),
        out_specs=[VM] * len(outs),
        scratch_shapes=list(scratch),
        compiler_params=pltpu.CompilerParams(vmem_limit_bytes=limit << 20),
    )

    def go(*args):
        near = [pltpu.with_memory_space_constraint(a, pltpu.VMEM) for a in args[smem:]]
        return run(*args[:smem], *near)

    return go


def norm_kernel(ids, x_ref, g_ref, o_ref):
    x = x_ref[...].astype(F32)
    scale = lax.rsqrt(jnp.mean(x * x, axis=-1, keepdims=True) + EPS)
    y = (x * scale * g_ref[...]).astype(BF)
    width = o_ref.shape[2]
    for b in range(o_ref.shape[0]):
        o_ref[ids[0] ^ b] = y[:, b * width:(b + 1) * width]


def qkv_kernel(g_ref, h_ref, w0_ref, w1_ref, *outs):
    width = w0_ref.shape[0]
    for d, o_ref in enumerate(outs):
        for kk, src in enumerate((g_ref, h_ref)):
            a = src[:, 2 * d].reshape(-1, width)
            b = src[:, 2 * d + 1].reshape(-1, width)
            acc = jnp.dot(a, w0_ref[...], preferred_element_type=F32)
            acc = acc + jnp.dot(b, w1_ref[...], preferred_element_type=F32)
            rows = acc.shape[0]
            o_ref[kk * rows:(kk + 1) * rows, :] = acc.astype(o_ref.dtype)


def place(row, section, step):
    group = row // step
    half = group // 8
    return (section ^ (2 * (group - 8 * half) + half)) * step + (row - group * step)


def attn_kernel(ids, own, r1, r2, r3, *rest):
    wo = rest[:8]
    outs = rest[8:10]
    packed = rest[10]
    mixed = rest[11]
    length = own.shape[0]
    packed[...] = (
        own[...] + r1[...].astype(F32) + r2[...].astype(F32) + r3[...].astype(F32)
    ).astype(BF)
    section = ids[1]
    valid = ids[2]
    rows = place(lax.broadcasted_iota(jnp.int32, (length, 1), 0), section, 16)
    cols = place(lax.broadcasted_iota(jnp.int32, (1, length), 1), section, 16)
    allowed = (cols <= rows) & (cols < valid)
    for h in range(own.shape[1] // (3 * HEAD)):
        base = h * 3 * HEAD
        q = packed[:, base:base + HEAD]
        k = packed[:, base + HEAD:base + 2 * HEAD]
        v = packed[:, base + 2 * HEAD:base + 3 * HEAD]
        s = lax.dot_general(q, k, (((1,), (1,)), ((), ())), preferred_element_type=F32)
        s = jnp.where(allowed, s * (1.0 / math.sqrt(HEAD)), NEG)
        top = jnp.max(s, axis=-1, keepdims=True)
        e = jnp.where(allowed, jnp.exp(s - top), 0.0)
        p = (e / jnp.sum(e, axis=-1, keepdims=True)).astype(BF)
        mixed[:, h * HEAD:(h + 1) * HEAD] = jnp.dot(
            p, v, preferred_element_type=F32
        ).astype(BF)
    half = length // 2
    width = wo[0].shape[1]
    for e in range(8):
        acc = jnp.dot(mixed[...], wo[e][...], preferred_element_type=F32).astype(BF)
        outs[0][:, e * width:(e + 1) * width] = acc[:half]
        outs[1][:, e * width:(e + 1) * width] = acc[half:]


def pair_kernel(a_ref, b_ref, *outs):
    for j, o_ref in enumerate(outs):
        rows = o_ref.shape[0]
        part = a_ref[j * rows:(j + 1) * rows, :].astype(F32) + b_ref[
            j * rows:(j + 1) * rows, :
        ].astype(F32)
        o_ref[...] = part.astype(o_ref.dtype)


def hidden_kernel(ids, frames, gain, *rest):
    pieces = rest[:8]
    o_ref = rest[8]
    acc = rest[9]
    width = frames.shape[1] // 8
    for e in range(8):
        cut = slice(e * width, (e + 1) * width)
        part = pieces[0][:, cut].astype(F32)
        for piece in pieces[1:]:
            part = part + piece[:, cut].astype(F32)
        acc[ids[0] ^ e] = part
    total = jnp.zeros((frames.shape[0], 1), F32)
    for b in range(8):
        cut = slice(b * width, (b + 1) * width)
        hid = frames[:, cut].astype(F32) + acc[b]
        acc[b] = hid
        total = total + jnp.sum(hid * hid, axis=-1, keepdims=True)
    scale = lax.rsqrt(total / frames.shape[1] + EPS)
    for b in range(8):
        cut = slice(b * width, (b + 1) * width)
        o_ref[:, cut] = (acc[b] * scale * gain[:, cut]).astype(BF)


def lift_kernel(g_ref, h_ref, din, emb, gain, wqkv, *outs):
    width = g_ref.shape[2]
    parts = []
    for src in (g_ref, h_ref):
        parts.append(src[...].reshape(-1, width))
    x = jnp.concatenate(parts, axis=0)
    lifted = jnp.dot(x, din[...], preferred_element_type=F32) + emb[...].astype(F32)
    scale = lax.rsqrt(jnp.mean(lifted * lifted, axis=-1, keepdims=True) + EPS)
    dn = (lifted * scale * gain[...]).astype(BF)
    step = 1024
    for s in range(wqkv.shape[1] // step):
        cut = slice(s * step, (s + 1) * step)
        y = jnp.dot(dn, wqkv[:, cut], preferred_element_type=F32).astype(BF)
        for e in range(8):
            outs[e][0, :, cut] = y[e * 16:(e + 1) * 16]
            outs[e][1, :, cut] = y[128 + e * 16:128 + (e + 1) * 16]


def fetch_kernel(*refs):
    sems = refs[-1]
    half = (len(refs) - 1) // 2
    copies = [
        pltpu.make_async_copy(refs[i], refs[half + i], sems.at[i]) for i in range(half)
    ]
    for copy in copies:
        copy.start()
    for copy in copies:
        copy.wait()


def fetch(*arrays):
    return pl.pallas_call(
        fetch_kernel,
        out_shape=[pltpu.VMEM(a.shape, a.dtype) for a in arrays],
        in_specs=[pl.BlockSpec(memory_space=pltpu.HBM)] * len(arrays),
        out_specs=[VM] * len(arrays),
        scratch_shapes=[pltpu.SemaphoreType.DMA((len(arrays),))],
        compiler_params=pltpu.CompilerParams(vmem_limit_bytes=1 << 20),
    )(*[pltpu.with_memory_space_constraint(a, pltpu.HBM) for a in arrays])


def depth_kernel(ids, *rest):
    pieces = rest[:8]
    other = rest[8]
    outs = rest[9:17]
    z = rest[17]
    for e in range(8):
        z[e * 16:(e + 1) * 16, :] = pieces[e][0]
        z[128 + e * 16:128 + (e + 1) * 16, :] = other[e]
    section = ids[1]
    rows = lax.broadcasted_iota(jnp.int32, (256, 1), 0)
    cols = lax.broadcasted_iota(jnp.int32, (1, 256), 1)
    rpos = place(rows, section, 16) // 16
    cpos = place(cols, section, 16) // 16
    keep = (cpos <= rpos) & (rows % 16 == cols % 16)
    bias = jnp.where(keep, 0.0, NEG)
    lane = lax.broadcasted_iota(jnp.int32, (256, 2 * DHEAD), 1)
    low = lane < DHEAD
    inner = z.shape[1] // 3
    for pair in range(inner // (2 * DHEAD)):
        base = pair * 2 * DHEAD
        q = z[:, base:base + 2 * DHEAD]
        k = z[:, inner + base:inner + base + 2 * DHEAD]
        v = z[:, 2 * inner + base:2 * inner + base + 2 * DHEAD]
        got = []
        for side in range(2):
            mask = low if side == 0 else jnp.logical_not(low)
            qs = jnp.where(mask, q, jnp.zeros_like(q))
            s = lax.dot_general(
                qs, k, (((1,), (1,)), ((), ())), preferred_element_type=F32
            )
            s = s * (1.0 / math.sqrt(DHEAD)) + bias
            top = jnp.max(s, axis=-1, keepdims=True)
            e = jnp.exp(s - top)
            total = jnp.sum(e, axis=-1, keepdims=True)
            o = jnp.dot(e.astype(BF), v, preferred_element_type=F32)
            got.append(o / total)
        res = jnp.where(low, got[0], got[1]).astype(BF)
        for e in range(8):
            outs[e][0, :, base:base + 2 * DHEAD] = res[e * 16:(e + 1) * 16]
            outs[e][1, :, base:base + 2 * DHEAD] = res[128 + e * 16:128 + (e + 1) * 16]


def final_kernel(ids, *rest):
    pieces = rest[:8]
    other = rest[8]
    o_ref = rest[9]
    for e in range(8):
        o_ref[ids[1] ^ (2 * e)] = pieces[e][0]
        o_ref[ids[1] ^ (2 * e + 1)] = other[e]


def gather(value):
    def cb(v, flip):
        return swap(v, "cb", 16, flip)

    y = cb(value, 8)
    x1 = cb(value, 2)
    x3 = cb(value, 6)
    x2 = cb(value, 4)
    y1 = cb(y, 2)
    y3 = cb(y, 6)
    y2 = cb(x2, 8)
    return [value, x1, x2, x3, y, y1, y2, y3]


def work(frames_in, valid_len, tokens, t_gain, w_qkv, w_out, h_gain, d_in, d_embed, d_gain, d_qkv):
    model = frames_in.shape[2]
    mine = frames_in[0]
    f = lax.axis_index("fsdp").astype(jnp.int32)
    c = lax.axis_index("cb").astype(jnp.int32)
    ids = jnp.stack([f, c, valid_len[0]])
    fs = lambda v, flip: swap(v, "fsdp", 8, flip)
    cb = lambda v, flip: swap(v, "cb", 16, flip)
    block = model // 8

    rel = call(norm_kernel, [((8, 16, block), BF)], smem=1, n_in=3)(
        ids, mine, t_gain[None]
    )[0]
    w_other = fs(w_qkv, 1)
    wo_other = fs(w_out, 1)
    local = [rel[0:2]] + [fs(rel[2 * d:2 * d + 2], 2 * d) for d in (1, 2, 3)]
    local = jnp.concatenate(local, axis=0)
    even = jnp.stack(gather(local))
    odd = cb(even, 1)
    cols = w_qkv.shape[1]
    parts = call(
        qkv_kernel, [((256, cols), F32)] + [((256, cols), BF)] * 3, n_in=4
    )(even, odd, w_qkv, w_other)
    wo_pair = jnp.stack([w_out, wo_other])
    wo_far = [fs(wo_pair, 2 * d) for d in (1, 2, 3)]
    wo = [w_out, wo_other]
    for pair in wo_far:
        wo += [pair[0], pair[1]]
    sums = [fs(parts[d], 2 * d) for d in (1, 2, 3)]
    keep, give = call(
        attn_kernel,
        [((128, model), BF)] * 2,
        scratch=[pltpu.VMEM((256, cols), BF), pltpu.VMEM((256, w_out.shape[0]), BF)],
        smem=1,
        n_in=13,
    )(ids, parts[0], *sums, *wo)
    taken = cb(give, 1)
    blocks = call(pair_kernel, [((16, model), F32)] + [((16, model), BF)] * 7, n_in=2)(
        keep, taken
    )
    pieces = [blocks[0]] + [cb(blocks[e], 2 * e) for e in range(1, 8)]
    hn = call(
        hidden_kernel,
        [((16, model), BF)],
        scratch=[pltpu.VMEM((8, 16, block), F32)],
        smem=1,
        n_in=11,
    )(ids, mine, h_gain[None], *pieces)[0]
    even = jnp.stack(gather(hn))
    odd = cb(even, 1)

    order = jnp.concatenate([2 * jnp.arange(8), 2 * jnp.arange(8) + 1]).astype(jnp.int32)
    ids_rel = tokens[0, 0].reshape(16, 16).at[c ^ order].get(mode="promise_in_bounds")
    emb = d_embed[0].at[ids_rel.reshape(256)].get(mode="promise_in_bounds")
    din, dqkv = fetch(d_in[0], d_qkv[0])
    inner = d_in.shape[2]
    sent = call(lift_kernel, [((2, 16, 3 * inner), BF)] * 8, n_in=6)(
        even, odd, din, emb, d_gain, dqkv
    )
    pieces = [sent[0]] + [cb(sent[e], 2 * e) for e in range(1, 8)]
    other = cb(jnp.stack([p[1] for p in pieces]), 1)
    outs = call(
        depth_kernel,
        [((2, 16, inner), BF)] * 8,
        scratch=[pltpu.VMEM((256, 3 * inner), BF)],
        smem=1,
        n_in=10,
    )(ids, *pieces, other)
    pieces = [outs[0]] + [cb(outs[e], 2 * e) for e in range(1, 8)]
    other = cb(jnp.stack([p[1] for p in pieces]), 1)
    out = call(final_kernel, [((16, 16, inner), BF)], smem=1, n_in=10, last=True)(
        ids, *pieces, other
    )[0]
    return out.reshape(1, 1, 256, inner)


def solution(mesh):
    placed = (
        P("fsdp", "cb", None),
        P("fsdp"),
        P("fsdp", "cb", None),
        P(),
        P("fsdp", "cb"),
        P("cb", "fsdp"),
        P(),
        P("cb", None, None),
        P("cb", None, None),
        P("cb", None),
        P("cb", None, None),
    )
    return jax.shard_map(
        work, mesh=mesh, in_specs=placed, out_specs=P("fsdp", "cb", None, None), check_vma=False
    )
```

```python
import math

import jax
import jax.numpy as jnp
from jax import lax
from jax.experimental import pallas as pl
from jax.experimental.pallas import tpu as pltpu
from jax.sharding import PartitionSpec as P


HEAD = 128
DHEAD = 64
EPS = 1e-05
NEG = -1e30
BF = jnp.bfloat16
F32 = jnp.float32


VM = pl.BlockSpec(memory_space=pltpu.VMEM)
SM = pl.BlockSpec(memory_space=pltpu.SMEM)


def swap(value, axis, size, flip):
    return lax.ppermute(value, axis, [(i, i ^ flip) for i in range(size)])


def call(kernel, outs, scratch=(), smem=0, n_in=0, limit=8, last=False):
    kind = jax.ShapeDtypeStruct if last else pltpu.VMEM
    run = pl.pallas_call(
        kernel,
        out_shape=[kind(s, d) for s, d in outs],
        in_specs=[SM] * smem + [VM] * (n_in - smem),
        out_specs=[VM] * len(outs),
        scratch_shapes=list(scratch),
        compiler_params=pltpu.CompilerParams(vmem_limit_bytes=limit << 20),
    )

    def go(*args):
        near = [pltpu.with_memory_space_constraint(a, pltpu.VMEM) for a in args[smem:]]
        return run(*args[:smem], *near)

    return go


def norm_kernel(ids, x_ref, g_ref, o_ref):
    x = x_ref[...].astype(F32)
    scale = lax.rsqrt(jnp.mean(x * x, axis=-1, keepdims=True) + EPS)
    y = (x * scale * g_ref[...]).astype(BF)
    width = o_ref.shape[2]
    for b in range(o_ref.shape[0]):
        o_ref[ids[0] ^ b] = y[:, b * width:(b + 1) * width]


def qkv_kernel(g_ref, h_ref, w0_ref, w1_ref, w2_ref, *outs):
    width = w0_ref.shape[0]
    half = width // 2
    for d, o_ref in enumerate(outs):
        for kk, src in enumerate((g_ref, h_ref)):
            a = src[:, 2 * d].reshape(-1, width)
            b = src[:, 2 * d + 1].reshape(-1, width)
            acc = jnp.dot(a, w0_ref[...], preferred_element_type=F32)
            acc = acc + jnp.dot(b[:, :half], w1_ref[...], preferred_element_type=F32)
            acc = acc + jnp.dot(b[:, half:], w2_ref[...], preferred_element_type=F32)
            rows = acc.shape[0]
            o_ref[kk * rows:(kk + 1) * rows, :] = acc.astype(o_ref.dtype)


def place(row, section, step):
    group = row // step
    half = group // 8
    return (section ^ (2 * (group - 8 * half) + half)) * step + (row - group * step)


def attn_kernel(ids, own, r1, r2, r3, *rest):
    wo = rest[:8]
    outs = rest[8:10]
    packed = rest[10]
    mixed = rest[11]
    length = own.shape[0]
    packed[...] = (
        own[...] + r1[...].astype(F32) + r2[...].astype(F32) + r3[...].astype(F32)
    ).astype(BF)
    section = ids[1]
    valid = ids[2]
    rows = place(lax.broadcasted_iota(jnp.int32, (length, 1), 0), section, 16)
    cols = place(lax.broadcasted_iota(jnp.int32, (1, length), 1), section, 16)
    allowed = (cols <= rows) & (cols < valid)
    for h in range(own.shape[1] // (3 * HEAD)):
        base = h * 3 * HEAD
        q = packed[:, base:base + HEAD]
        k = packed[:, base + HEAD:base + 2 * HEAD]
        v = packed[:, base + 2 * HEAD:base + 3 * HEAD]
        s = lax.dot_general(q, k, (((1,), (1,)), ((), ())), preferred_element_type=F32)
        s = jnp.where(allowed, s * (1.0 / math.sqrt(HEAD)), NEG)
        top = jnp.max(s, axis=-1, keepdims=True)
        e = jnp.where(allowed, jnp.exp(s - top), 0.0)
        p = (e / jnp.sum(e, axis=-1, keepdims=True)).astype(BF)
        mixed[:, h * HEAD:(h + 1) * HEAD] = jnp.dot(
            p, v, preferred_element_type=F32
        ).astype(BF)
    half = length // 2
    width = wo[0].shape[1]
    for e in range(8):
        acc = jnp.dot(mixed[...], wo[e][...], preferred_element_type=F32).astype(BF)
        outs[0][:, e * width:(e + 1) * width] = acc[:half]
        outs[1][:, e * width:(e + 1) * width] = acc[half:]


def pair_kernel(a_ref, b_ref, *outs):
    for j, o_ref in enumerate(outs):
        rows = o_ref.shape[0]
        part = a_ref[j * rows:(j + 1) * rows, :].astype(F32) + b_ref[
            j * rows:(j + 1) * rows, :
        ].astype(F32)
        o_ref[...] = part.astype(o_ref.dtype)


def hidden_kernel(ids, frames, gain, *rest):
    pieces = rest[:5]
    o_ref = rest[5]
    acc = rest[6]
    width = frames.shape[1] // 8
    for e in range(8):
        cut = slice(e * width, (e + 1) * width)
        part = pieces[0][:, cut].astype(F32)
        for piece in pieces[1:]:
            part = part + piece[:, cut].astype(F32)
        acc[ids[0] ^ e] = part
    total = jnp.zeros((frames.shape[0], 1), F32)
    for b in range(8):
        cut = slice(b * width, (b + 1) * width)
        hid = frames[:, cut].astype(F32) + acc[b]
        acc[b] = hid
        total = total + jnp.sum(hid * hid, axis=-1, keepdims=True)
    scale = lax.rsqrt(total / frames.shape[1] + EPS)
    for b in range(8):
        cut = slice(b * width, (b + 1) * width)
        o_ref[:, cut] = (acc[b] * scale * gain[:, cut]).astype(BF)


def lift_kernel(g_ref, h_ref, din, emb, gain, wqkv, *outs):
    width = g_ref.shape[2]
    parts = []
    for src in (g_ref, h_ref):
        parts.append(src[...].reshape(-1, width))
    x = jnp.concatenate(parts, axis=0)
    lifted = jnp.dot(x, din[...], preferred_element_type=F32) + emb[...].astype(F32)
    scale = lax.rsqrt(jnp.mean(lifted * lifted, axis=-1, keepdims=True) + EPS)
    dn = (lifted * scale * gain[...]).astype(BF)
    step = 1024
    for s in range(wqkv.shape[1] // step):
        cut = slice(s * step, (s + 1) * step)
        y = jnp.dot(dn, wqkv[:, cut], preferred_element_type=F32).astype(BF)
        for e in range(8):
            outs[e][0, :, cut] = y[e * 16:(e + 1) * 16]
            outs[e][1, :, cut] = y[128 + e * 16:128 + (e + 1) * 16]


def fetch_kernel(*refs):
    sems = refs[-1]
    half = (len(refs) - 1) // 2
    copies = [
        pltpu.make_async_copy(refs[i], refs[half + i], sems.at[i]) for i in range(half)
    ]
    for copy in copies:
        copy.start()
    for copy in copies:
        copy.wait()


def fetch(*arrays):
    return pl.pallas_call(
        fetch_kernel,
        out_shape=[pltpu.VMEM(a.shape, a.dtype) for a in arrays],
        in_specs=[pl.BlockSpec(memory_space=pltpu.HBM)] * len(arrays),
        out_specs=[VM] * len(arrays),
        scratch_shapes=[pltpu.SemaphoreType.DMA((len(arrays),))],
        compiler_params=pltpu.CompilerParams(vmem_limit_bytes=1 << 20),
    )(*[pltpu.with_memory_space_constraint(a, pltpu.HBM) for a in arrays])


def depth_kernel(ids, *rest):
    pieces = rest[:8]
    other = rest[8]
    outs = rest[9:17]
    z = rest[17]
    for e in range(8):
        z[e * 16:(e + 1) * 16, :] = pieces[e][0]
        z[128 + e * 16:128 + (e + 1) * 16, :] = other[e]
    section = ids[1]
    rows = lax.broadcasted_iota(jnp.int32, (256, 1), 0)
    cols = lax.broadcasted_iota(jnp.int32, (1, 256), 1)
    rpos = place(rows, section, 16) // 16
    cpos = place(cols, section, 16) // 16
    keep = (cpos <= rpos) & (rows % 16 == cols % 16)
    bias = jnp.where(keep, 0.0, NEG)
    lane = lax.broadcasted_iota(jnp.int32, (256, 2 * DHEAD), 1)
    low = lane < DHEAD
    inner = z.shape[1] // 3
    for pair in range(inner // (2 * DHEAD)):
        base = pair * 2 * DHEAD
        q = z[:, base:base + 2 * DHEAD]
        k = z[:, inner + base:inner + base + 2 * DHEAD]
        v = z[:, 2 * inner + base:2 * inner + base + 2 * DHEAD]
        got = []
        for side in range(2):
            mask = low if side == 0 else jnp.logical_not(low)
            qs = jnp.where(mask, q, jnp.zeros_like(q))
            s = lax.dot_general(
                qs, k, (((1,), (1,)), ((), ())), preferred_element_type=F32
            )
            s = s * (1.0 / math.sqrt(DHEAD)) + bias
            top = jnp.max(s, axis=-1, keepdims=True)
            e = jnp.exp(s - top)
            total = jnp.sum(e, axis=-1, keepdims=True)
            o = jnp.dot(e.astype(BF), v, preferred_element_type=F32)
            got.append(o / total)
        res = jnp.where(low, got[0], got[1]).astype(BF)
        for e in range(8):
            outs[e][0, :, base:base + 2 * DHEAD] = res[e * 16:(e + 1) * 16]
            outs[e][1, :, base:base + 2 * DHEAD] = res[128 + e * 16:128 + (e + 1) * 16]


def final_kernel(ids, *rest):
    pieces = rest[:8]
    other = rest[8]
    o_ref = rest[9]
    for e in range(8):
        o_ref[ids[1] ^ (2 * e)] = pieces[e][0]
        o_ref[ids[1] ^ (2 * e + 1)] = other[e]


def add_kernel(*refs):
    part = refs[0][...].astype(F32)
    for ref in refs[1:-1]:
        part = part + ref[...].astype(F32)
    refs[-1][...] = part.astype(BF)


def add(*values):
    return call(add_kernel, [(values[0].shape, BF)], n_in=len(values), limit=2)(*values)[0]


def gather(value, across=False):
    def cb(v, flip):
        return swap(v, "cb", 16, flip)

    y = cb(value, 8)
    x1 = cb(value, 2)
    x3 = cb(value, 6)
    x2 = cb(value, 4)
    y1 = cb(y, 2)
    y3 = cb(y, 6)
    y2 = cb(y, 4) if across else cb(x2, 8)
    return [value, x1, x2, x3, y, y1, y2, y3]


def work(frames_in, valid_len, tokens, t_gain, w_qkv, w_out, h_gain, d_in, d_embed, d_gain, d_qkv):
    model = frames_in.shape[2]
    mine = frames_in[0]
    f = lax.axis_index("fsdp").astype(jnp.int32)
    c = lax.axis_index("cb").astype(jnp.int32)
    ids = jnp.stack([f, c, valid_len[0]])
    fs = lambda v, flip: swap(v, "fsdp", 8, flip)
    cb = lambda v, flip: swap(v, "cb", 16, flip)
    block = model // 8

    rel = call(norm_kernel, [((8, 16, block), BF)], smem=1, n_in=3)(
        ids, mine, t_gain[None]
    )[0]
    rows = w_qkv.shape[0] // 2
    w_other0 = fs(w_qkv[:rows], 1)
    w_other1 = fs(w_qkv[rows:], 1)
    local = [rel[0:2]] + [fs(rel[2 * d:2 * d + 2], 2 * d) for d in (1, 2, 3)]
    local = jnp.concatenate(local, axis=0)
    wo_even = [w_out] + [fs(w_out, 2 * d) for d in (1, 2, 3)]
    wo_odd = [fs(w, 1) for w in wo_even]
    wo = [w for pair in zip(wo_even, wo_odd) for w in pair]
    even = jnp.stack(gather(local, True))
    odd = cb(even, 1)
    cols = w_qkv.shape[1]
    parts = call(
        qkv_kernel, [((256, cols), F32)] + [((256, cols), BF)] * 3, n_in=5
    )(even, odd, w_qkv, w_other0, w_other1)
    sums = [fs(parts[d], 2 * d) for d in (1, 2, 3)]
    keep, give = call(
        attn_kernel,
        [((128, model), BF)] * 2,
        scratch=[pltpu.VMEM((256, cols), BF), pltpu.VMEM((256, w_out.shape[0]), BF)],
        smem=1,
        n_in=13,
    )(ids, parts[0], *sums, *wo)
    taken = cb(give, 1)
    blocks = call(pair_kernel, [((16, model), F32)] + [((16, model), BF)] * 7, n_in=2)(
        keep, taken
    )
    far1, far3 = cb(blocks[5], 2), cb(blocks[7], 6)
    far2 = cb(blocks[6], 8)
    near1, near3 = cb(blocks[1], 2), cb(blocks[3], 6)
    side = add(blocks[4], far1, far3)
    deep = add(blocks[2], far2)
    pieces = [blocks[0], near1, near3, cb(side, 8), cb(deep, 4)]
    hn = call(
        hidden_kernel,
        [((16, model), BF)],
        scratch=[pltpu.VMEM((8, 16, block), F32)],
        smem=1,
        n_in=8,
    )(ids, mine, h_gain[None], *pieces)[0]
    even = jnp.stack(gather(hn))
    odd = cb(even, 1)

    order = jnp.concatenate([2 * jnp.arange(8), 2 * jnp.arange(8) + 1]).astype(jnp.int32)
    ids_rel = tokens[0, 0].reshape(16, 16).at[c ^ order].get(mode="promise_in_bounds")
    emb = d_embed[0].at[ids_rel.reshape(256)].get(mode="promise_in_bounds")
    din, dqkv = fetch(d_in[0], d_qkv[0])
    inner = d_in.shape[2]
    sent = call(lift_kernel, [((2, 16, 3 * inner), BF)] * 8, n_in=6)(
        even, odd, din, emb, d_gain, dqkv
    )
    pieces = [sent[0]] + [cb(sent[e], 2 * e) for e in range(1, 8)]
    other = cb(jnp.stack([p[1] for p in pieces]), 1)
    outs = call(
        depth_kernel,
        [((2, 16, inner), BF)] * 8,
        scratch=[pltpu.VMEM((256, 3 * inner), BF)],
        smem=1,
        n_in=10,
    )(ids, *pieces, other)
    pieces = [outs[0]] + [cb(outs[e], 2 * e) for e in range(1, 8)]
    other = cb(jnp.stack([p[1] for p in pieces]), 1)
    out = call(final_kernel, [((16, 16, inner), BF)], smem=1, n_in=10, last=True)(
        ids, *pieces, other
    )[0]
    return out.reshape(1, 1, 256, inner)


def solution(mesh):
    placed = (
        P("fsdp", "cb", None),
        P("fsdp"),
        P("fsdp", "cb", None),
        P(),
        P("fsdp", "cb"),
        P("cb", "fsdp"),
        P(),
        P("cb", None, None),
        P("cb", None, None),
        P("cb", None),
        P("cb", None, None),
    )
    return jax.shard_map(
        work, mesh=mesh, in_specs=placed, out_specs=P("fsdp", "cb", None, None), check_vma=False
    )
```

```python
import functools
import math

import jax
import jax.numpy as jnp
from jax import lax
from jax.experimental import pallas as pl
from jax.experimental.pallas import tpu as pltpu
from jax.sharding import PartitionSpec as P


HEAD = 128
DHEAD = 64
EPS = 1e-05
NEG = -1e30
BF = jnp.bfloat16
F32 = jnp.float32


VM = pl.BlockSpec(memory_space=pltpu.VMEM)
SM = pl.BlockSpec(memory_space=pltpu.SMEM)


def swap(value, axis, size, flip):
    return lax.ppermute(value, axis, [(i, i ^ flip) for i in range(size)])


def call(kernel, outs, scratch=(), smem=0, n_in=0, limit=8, last=False):
    kind = jax.ShapeDtypeStruct if last else pltpu.VMEM
    run = pl.pallas_call(
        kernel,
        out_shape=[kind(s, d) for s, d in outs],
        in_specs=[SM] * smem + [VM] * (n_in - smem),
        out_specs=[VM] * len(outs),
        scratch_shapes=list(scratch),
        compiler_params=pltpu.CompilerParams(vmem_limit_bytes=limit << 20),
    )

    def go(*args):
        near = [pltpu.with_memory_space_constraint(a, pltpu.VMEM) for a in args[smem:]]
        return run(*args[:smem], *near)

    return go


def norm_kernel(ids, x_ref, g_ref, o_ref):
    x = x_ref[...].astype(F32)
    scale = lax.rsqrt(jnp.mean(x * x, axis=-1, keepdims=True) + EPS)
    y = (x * scale * g_ref[...]).astype(BF)
    width = o_ref.shape[2]
    for b in range(o_ref.shape[0]):
        o_ref[ids[0] ^ b] = y[:, b * width:(b + 1) * width]


def qkv_kernel(src, w0_ref, w1_ref, *outs):
    width = w0_ref.shape[0]
    for d, o_ref in enumerate(outs):
        a = src[:, 2 * d].reshape(-1, width)
        b = src[:, 2 * d + 1].reshape(-1, width)
        acc = jnp.dot(a, w0_ref[...], preferred_element_type=F32)
        acc = acc + jnp.dot(b, w1_ref[...], preferred_element_type=F32)
        o_ref[...] = acc.astype(o_ref.dtype)


def place(row, section, step):
    group = row // step
    half = group // 8
    return (section ^ (2 * (group - 8 * half) + half)) * step + (row - group * step)


def attn_kernel(ids, a0, a1, a2, b0, b1, b2, *rest):
    wo = rest[:8]
    outs = rest[8:10]
    packed = rest[10]
    mixed = rest[11]
    length, width = packed.shape
    half = length // 2
    for at, trio in ((0, (a0, a1, a2)), (half, (b0, b1, b2))):
        part = trio[0][...] + trio[1][...].astype(F32) + trio[2][...].astype(F32)
        packed[at:at + half, :] = part.astype(BF)
    section = ids[1]
    valid = ids[2]
    rows = place(lax.broadcasted_iota(jnp.int32, (length, 1), 0), section, 16)
    cols = place(lax.broadcasted_iota(jnp.int32, (1, length), 1), section, 16)
    allowed = (cols <= rows) & (cols < valid)
    for h in range(width // (3 * HEAD)):
        base = h * 3 * HEAD
        q = packed[:, base:base + HEAD]
        k = packed[:, base + HEAD:base + 2 * HEAD]
        v = packed[:, base + 2 * HEAD:base + 3 * HEAD]
        s = lax.dot_general(q, k, (((1,), (1,)), ((), ())), preferred_element_type=F32)
        s = jnp.where(allowed, s * (1.0 / math.sqrt(HEAD)), NEG)
        top = jnp.max(s, axis=-1, keepdims=True)
        e = jnp.where(allowed, jnp.exp(s - top), 0.0)
        p = (e / jnp.sum(e, axis=-1, keepdims=True)).astype(BF)
        mixed[:, h * HEAD:(h + 1) * HEAD] = jnp.dot(
            p, v, preferred_element_type=F32
        ).astype(BF)
    width = wo[0].shape[1]
    for e in range(8):
        acc = jnp.dot(mixed[...], wo[e][...], preferred_element_type=F32).astype(BF)
        outs[0][:, e * width:(e + 1) * width] = acc[:half]
        outs[1][:, e * width:(e + 1) * width] = acc[half:]


def pair_kernel(a_ref, b_ref, *outs):
    for j, o_ref in enumerate(outs):
        rows = o_ref.shape[0]
        part = a_ref[j * rows:(j + 1) * rows, :].astype(F32) + b_ref[
            j * rows:(j + 1) * rows, :
        ].astype(F32)
        o_ref[...] = part.astype(o_ref.dtype)


def hidden_kernel(ids, frames, gain, *rest):
    pieces = rest[:5]
    o_ref = rest[5]
    acc = rest[6]
    width = frames.shape[1] // 8
    for e in range(8):
        cut = slice(e * width, (e + 1) * width)
        part = pieces[0][:, cut].astype(F32)
        for piece in pieces[1:]:
            part = part + piece[:, cut].astype(F32)
        acc[ids[0] ^ e] = part
    total = jnp.zeros((frames.shape[0], 1), F32)
    for b in range(8):
        cut = slice(b * width, (b + 1) * width)
        hid = frames[:, cut].astype(F32) + acc[b]
        acc[b] = hid
        total = total + jnp.sum(hid * hid, axis=-1, keepdims=True)
    scale = lax.rsqrt(total / frames.shape[1] + EPS)
    for b in range(8):
        cut = slice(b * width, (b + 1) * width)
        o_ref[:, cut] = (acc[b] * scale * gain[:, cut]).astype(BF)


def lift_kernel(row, src, din, emb, gain, wqkv, *outs):
    x = src[...].reshape(-1, src.shape[2])
    near = emb[row:row + x.shape[0], :].astype(F32)
    lifted = jnp.dot(x, din[...], preferred_element_type=F32) + near
    scale = lax.rsqrt(jnp.mean(lifted * lifted, axis=-1, keepdims=True) + EPS)
    dn = (lifted * scale * gain[...]).astype(BF)
    step = 1024
    for s in range(wqkv.shape[1] // step):
        cut = slice(s * step, (s + 1) * step)
        y = jnp.dot(dn, wqkv[:, cut], preferred_element_type=F32).astype(BF)
        for e in range(8):
            if len(outs) == 8:
                outs[e][:, cut] = y[e * 16:(e + 1) * 16]
            else:
                outs[0][e, :, cut] = y[e * 16:(e + 1) * 16]


def fetch_kernel(picks, din, dqkv, table, din_o, dqkv_o, rows_o, near, sems):
    moves = ((table, near), (din, din_o), (dqkv, dqkv_o))
    copies = [
        pltpu.make_async_copy(src, dst, sems.at[i]) for i, (src, dst) in enumerate(moves)
    ]
    for copy in copies:
        copy.start()
    copies[0].wait()
    count = near.shape[0]
    lane = lax.broadcasted_iota(jnp.int32, (picks.shape[0], count), 1)
    hot = jnp.where(lane == picks[...], 1.0, 0.0).astype(BF)
    rows_o[...] = jnp.dot(hot, near[...], preferred_element_type=F32).astype(BF)
    copies[1].wait()
    copies[2].wait()


def fetch(picks, din, dqkv, table):
    far = pl.BlockSpec(memory_space=pltpu.HBM)
    shapes = [din.shape, dqkv.shape, (picks.shape[0], table.shape[1])]
    big = [pltpu.with_memory_space_constraint(a, pltpu.HBM) for a in (din, dqkv, table)]
    return pl.pallas_call(
        fetch_kernel,
        out_shape=[pltpu.VMEM(s, BF) for s in shapes],
        in_specs=[VM, far, far, far],
        out_specs=[VM] * 3,
        scratch_shapes=[pltpu.VMEM(table.shape, BF), pltpu.SemaphoreType.DMA((3,))],
        compiler_params=pltpu.CompilerParams(vmem_limit_bytes=14 << 20),
    )(pltpu.with_memory_space_constraint(picks, pltpu.VMEM), *big)


def depth_kernel(ids, *rest):
    outs = rest[16:24]
    z = rest[24]
    for m in range(16):
        z[m * 16:(m + 1) * 16, :] = rest[m][...]
    section = ids[1]
    rows = lax.broadcasted_iota(jnp.int32, (256, 1), 0)
    cols = lax.broadcasted_iota(jnp.int32, (1, 256), 1)
    rpos = place(rows, section, 16) // 16
    cpos = place(cols, section, 16) // 16
    keep = (cpos <= rpos) & (rows % 16 == cols % 16)
    bias = jnp.where(keep, 0.0, NEG)
    lane = lax.broadcasted_iota(jnp.int32, (256, 2 * DHEAD), 1)
    low = lane < DHEAD
    inner = z.shape[1] // 3
    for pair in range(inner // (2 * DHEAD)):
        base = pair * 2 * DHEAD
        q = z[:, base:base + 2 * DHEAD]
        k = z[:, inner + base:inner + base + 2 * DHEAD]
        v = z[:, 2 * inner + base:2 * inner + base + 2 * DHEAD]
        got = []
        for side in range(2):
            mask = low if side == 0 else jnp.logical_not(low)
            qs = jnp.where(mask, q, jnp.zeros_like(q))
            s = lax.dot_general(
                qs, k, (((1,), (1,)), ((), ())), preferred_element_type=F32
            )
            s = s * (1.0 / math.sqrt(DHEAD)) + bias
            top = jnp.max(s, axis=-1, keepdims=True)
            e = jnp.exp(s - top)
            total = jnp.sum(e, axis=-1, keepdims=True)
            o = jnp.dot(e.astype(BF), v, preferred_element_type=F32)
            got.append(o / total)
        res = jnp.where(low, got[0], got[1]).astype(BF)
        for e in range(8):
            outs[e][0, :, base:base + 2 * DHEAD] = res[e * 16:(e + 1) * 16]
            outs[e][1, :, base:base + 2 * DHEAD] = res[128 + e * 16:128 + (e + 1) * 16]


def final_kernel(ids, *rest):
    pieces = rest[:8]
    other = rest[8]
    o_ref = rest[9]
    for e in range(8):
        o_ref[ids[1] ^ (2 * e)] = pieces[e][0]
        o_ref[ids[1] ^ (2 * e + 1)] = other[e]


def add_kernel(*refs):
    part = refs[0][...].astype(F32)
    for ref in refs[1:-1]:
        part = part + ref[...].astype(F32)
    refs[-1][...] = part.astype(BF)


def add(*values):
    return call(add_kernel, [(values[0].shape, BF)], n_in=len(values), limit=2)(*values)[0]


def gather(value, across=False):
    def cb(v, flip):
        return swap(v, "cb", 16, flip)

    y = cb(value, 8)
    x1 = cb(value, 2)
    x3 = cb(value, 6)
    x2 = cb(value, 4)
    y1 = cb(y, 2)
    y3 = cb(y, 6)
    y2 = cb(y, 4) if across else cb(x2, 8)
    return [value, x1, x2, x3, y, y1, y2, y3]


def work(frames_in, valid_len, tokens, t_gain, w_qkv, w_out, h_gain, d_in, d_embed, d_gain, d_qkv):
    model = frames_in.shape[2]
    mine = frames_in[0]
    f = lax.axis_index("fsdp").astype(jnp.int32)
    c = lax.axis_index("cb").astype(jnp.int32)
    ids = jnp.stack([f, c, valid_len[0]])
    fs = lambda v, flip: swap(v, "fsdp", 8, flip)
    cb = lambda v, flip: swap(v, "cb", 16, flip)
    block = model // 8

    rel = call(norm_kernel, [((8, 16, block), BF)], smem=1, n_in=3)(
        ids, mine, t_gain[None]
    )[0]
    near = fs(w_out, 1)
    w_other = fs(w_qkv, 1)
    local = [rel[0:2]] + [fs(rel[2 * d:2 * d + 2], 2 * d) for d in (1, 2, 3)]
    local = jnp.concatenate(local, axis=0)
    wo_even = [w_out] + [fs(w_out, 2 * d) for d in (1, 2, 3)]
    wo_odd = [near] + [fs(w, 1) for w in wo_even[1:]]
    wo = [w for pair in zip(wo_even, wo_odd) for w in pair]
    even = jnp.stack(gather(local, True))
    odd = cb(even, 1)
    cols = w_qkv.shape[1]

    def project(src, kinds):
        return call(qkv_kernel, [((128, cols), k) for k in kinds], n_in=3)(
            src, w_qkv, w_other
        )

    a0, a1, a2, a3 = project(even, (F32, BF, BF, F32))
    relay_a = fs(a2, 2)
    plain_a = fs(a1, 2)
    b0, b1, b2, b3 = project(odd, (F32, F32, BF, BF))
    relay_b = fs(b2, 6)
    plain_b = fs(b3, 6)
    sum_a = fs(add(a3, relay_a), 6)
    sum_b = fs(add(b1, relay_b), 2)
    keep, give = call(
        attn_kernel,
        [((128, model), BF)] * 2,
        scratch=[pltpu.VMEM((256, cols), BF), pltpu.VMEM((256, w_out.shape[0]), BF)],
        smem=1,
        n_in=15,
    )(ids, a0, plain_a, sum_a, b0, plain_b, sum_b, *wo)
    taken = cb(give, 1)
    blocks = call(pair_kernel, [((16, model), F32)] + [((16, model), BF)] * 7, n_in=2)(
        keep, taken
    )
    far1, far3 = cb(blocks[5], 2), cb(blocks[7], 6)
    far2 = cb(blocks[6], 8)
    near1, near3 = cb(blocks[1], 2), cb(blocks[3], 6)
    side = add(blocks[4], far1, far3)
    deep = add(blocks[2], far2)
    pieces = [blocks[0], near1, near3, cb(side, 8), cb(deep, 4)]
    hn = call(
        hidden_kernel,
        [((16, model), BF)],
        scratch=[pltpu.VMEM((8, 16, block), F32)],
        smem=1,
        n_in=8,
    )(ids, mine, h_gain[None], *pieces)[0]
    even = jnp.stack(gather(hn))
    odd = cb(even, 1)

    order = jnp.concatenate([2 * jnp.arange(8), 2 * jnp.arange(8) + 1]).astype(jnp.int32)
    mine_at = (jnp.arange(16, dtype=jnp.int32)[None, :] == (c ^ order)[:, None])[:, :, None]
    picks = jnp.sum(jnp.where(mine_at, tokens[0, 0].reshape(1, 16, 16), 0), axis=1)
    din, dqkv, emb = fetch(picks.reshape(256, 1), d_in[0], d_qkv[0], d_embed[0])
    inner = d_in.shape[2]

    def lift(src, row, outs):
        return call(functools.partial(lift_kernel, row), outs, n_in=5, limit=12)(
            src, din, emb, d_gain, dqkv
        )

    low = lift(even, 0, [((16, 3 * inner), BF)] * 8)
    high = lift(odd, 128, [((8, 16, 3 * inner), BF)])[0]
    high = cb(high, 1)
    got = {e: cb(low[e], 2 * e) for e in (1, 2, 3)}
    got.update({e: cb(low[e], 2 * e) for e in (4, 5, 6, 7)})
    deep = [high[0]] + [cb(high[e], 2 * e) for e in range(1, 8)]
    pieces = [low[0]] + [got[e] for e in range(1, 8)] + deep
    outs = call(
        depth_kernel,
        [((2, 16, inner), BF)] * 8,
        scratch=[pltpu.VMEM((256, 3 * inner), BF)],
        smem=1,
        n_in=17,
    )(ids, *pieces)
    pieces = [outs[0]] + [cb(outs[e], 2 * e) for e in range(1, 8)]
    other = cb(jnp.stack([p[1] for p in pieces]), 1)
    out = call(final_kernel, [((16, 16, inner), BF)], smem=1, n_in=10, last=True)(
        ids, *pieces, other
    )[0]
    return out.reshape(1, 1, 256, inner)


def solution(mesh):
    placed = (
        P("fsdp", "cb", None),
        P("fsdp"),
        P("fsdp", "cb", None),
        P(),
        P("fsdp", "cb"),
        P("cb", "fsdp"),
        P(),
        P("cb", None, None),
        P("cb", None, None),
        P("cb", None),
        P("cb", None, None),
    )
    return jax.shard_map(
        work, mesh=mesh, in_specs=placed, out_specs=P("fsdp", "cb", None, None), check_vma=False
    )
```

```python
import functools
import math

import jax
import jax.numpy as jnp
from jax import lax
from jax.experimental import pallas as pl
from jax.experimental.pallas import tpu as pltpu
from jax.sharding import PartitionSpec as P


HEAD = 128
DHEAD = 64
EPS = 1e-05
NEG = -1e30
BF = jnp.bfloat16
F32 = jnp.float32


VM = pl.BlockSpec(memory_space=pltpu.VMEM)
SM = pl.BlockSpec(memory_space=pltpu.SMEM)


def swap(value, axis, size, flip):
    return lax.ppermute(value, axis, [(i, i ^ flip) for i in range(size)])


def call(kernel, outs, scratch=(), smem=0, n_in=0, limit=8, last=False):
    kind = jax.ShapeDtypeStruct if last else pltpu.VMEM
    run = pl.pallas_call(
        kernel,
        out_shape=[kind(s, d) for s, d in outs],
        in_specs=[SM] * smem + [VM] * (n_in - smem),
        out_specs=[VM] * len(outs),
        scratch_shapes=list(scratch),
        compiler_params=pltpu.CompilerParams(vmem_limit_bytes=limit << 20),
    )

    def go(*args):
        near = [pltpu.with_memory_space_constraint(a, pltpu.VMEM) for a in args[smem:]]
        return run(*args[:smem], *near)

    return go


def norm_kernel(ids, x_ref, g_ref, o_ref):
    x = x_ref[...].astype(F32)
    scale = lax.rsqrt(jnp.mean(x * x, axis=-1, keepdims=True) + EPS)
    y = (x * scale * g_ref[...]).astype(BF)
    width = o_ref.shape[2]
    for b in range(o_ref.shape[0]):
        o_ref[ids[0] ^ b] = y[:, b * width:(b + 1) * width]


def qkv_kernel(src, w0_ref, w1_ref, *outs):
    width = w0_ref.shape[0]
    for d, o_ref in enumerate(outs):
        a = src[:, 2 * d].reshape(-1, width)
        b = src[:, 2 * d + 1].reshape(-1, width)
        acc = jnp.dot(a, w0_ref[...], preferred_element_type=F32)
        acc = acc + jnp.dot(b, w1_ref[...], preferred_element_type=F32)
        o_ref[...] = acc.astype(o_ref.dtype)


def place(row, section, step):
    group = row // step
    half = group // 8
    return (section ^ (2 * (group - 8 * half) + half)) * step + (row - group * step)


def attn_kernel(ids, a0, a1, a2, b0, b1, b2, *rest):
    wo = rest[:8]
    give, left = rest[8:10]
    packed = rest[10]
    mixed = rest[11]
    length, width = packed.shape
    half = length // 2
    for at, trio in ((0, (a0, a1, a2)), (half, (b0, b1, b2))):
        part = trio[0][...] + trio[1][...].astype(F32) + trio[2][...].astype(F32)
        packed[at:at + half, :] = part.astype(BF)
    section = ids[1]
    valid = ids[2]
    rows = place(lax.broadcasted_iota(jnp.int32, (length, 1), 0), section, 16)
    cols = place(lax.broadcasted_iota(jnp.int32, (1, length), 1), section, 16)
    allowed = (cols <= rows) & (cols < valid)
    for h in range(width // (3 * HEAD)):
        base = h * 3 * HEAD
        q = packed[:, base:base + HEAD]
        k = packed[:, base + HEAD:base + 2 * HEAD]
        v = packed[:, base + 2 * HEAD:base + 3 * HEAD]
        s = lax.dot_general(q, k, (((1,), (1,)), ((), ())), preferred_element_type=F32)
        s = jnp.where(allowed, s * (1.0 / math.sqrt(HEAD)), NEG)
        top = jnp.max(s, axis=-1, keepdims=True)
        e = jnp.where(allowed, jnp.exp(s - top), 0.0)
        p = (e / jnp.sum(e, axis=-1, keepdims=True)).astype(BF)
        mixed[:, h * HEAD:(h + 1) * HEAD] = jnp.dot(
            p, v, preferred_element_type=F32
        ).astype(BF)
    left[...] = mixed[:half, :]
    spread(mixed[half:, :], wo, give)


def spread(rows, wo, o_ref):
    width = wo[0].shape[1]
    for e in range(8):
        acc = jnp.dot(rows, wo[e][...], preferred_element_type=F32)
        o_ref[:, e * width:(e + 1) * width] = acc.astype(BF)


def keep_kernel(left, *rest):
    spread(left[...], rest[:8], rest[8])


def pair_kernel(a_ref, b_ref, *outs):
    for j, o_ref in enumerate(outs):
        rows = o_ref.shape[0]
        part = a_ref[j * rows:(j + 1) * rows, :].astype(F32) + b_ref[
            j * rows:(j + 1) * rows, :
        ].astype(F32)
        o_ref[...] = part.astype(o_ref.dtype)


def hidden_kernel(ids, frames, gain, *rest):
    pieces = rest[:5]
    o_ref = rest[5]
    acc = rest[6]
    width = frames.shape[1] // 8
    for e in range(8):
        cut = slice(e * width, (e + 1) * width)
        part = pieces[0][:, cut].astype(F32)
        for piece in pieces[1:]:
            part = part + piece[:, cut].astype(F32)
        acc[ids[0] ^ e] = part
    total = jnp.zeros((frames.shape[0], 1), F32)
    for b in range(8):
        cut = slice(b * width, (b + 1) * width)
        hid = frames[:, cut].astype(F32) + acc[b]
        acc[b] = hid
        total = total + jnp.sum(hid * hid, axis=-1, keepdims=True)
    scale = lax.rsqrt(total / frames.shape[1] + EPS)
    for b in range(8):
        cut = slice(b * width, (b + 1) * width)
        o_ref[:, cut] = (acc[b] * scale * gain[:, cut]).astype(BF)


def lift_kernel(row, src, din, emb, gain, wqkv, *outs):
    x = src[...].reshape(-1, src.shape[2])
    near = emb[row:row + x.shape[0], :].astype(F32)
    lifted = jnp.dot(x, din[...], preferred_element_type=F32) + near
    scale = lax.rsqrt(jnp.mean(lifted * lifted, axis=-1, keepdims=True) + EPS)
    dn = (lifted * scale * gain[...]).astype(BF)
    step = 1024
    for s in range(wqkv.shape[1] // step):
        cut = slice(s * step, (s + 1) * step)
        y = jnp.dot(dn, wqkv[:, cut], preferred_element_type=F32).astype(BF)
        for e in range(8):
            if len(outs) == 8:
                outs[e][:, cut] = y[e * 16:(e + 1) * 16]
            else:
                outs[0][e, :, cut] = y[e * 16:(e + 1) * 16]


def fetch_kernel(picks, din, dqkv, table, din_o, dqkv_o, rows_o, near, sems):
    moves = ((table, near), (din, din_o), (dqkv, dqkv_o))
    copies = [
        pltpu.make_async_copy(src, dst, sems.at[i]) for i, (src, dst) in enumerate(moves)
    ]
    for copy in copies:
        copy.start()
    copies[0].wait()
    count = near.shape[0]
    lane = lax.broadcasted_iota(jnp.int32, (picks.shape[0], count), 1)
    hot = jnp.where(lane == picks[...], 1.0, 0.0).astype(BF)
    rows_o[...] = jnp.dot(hot, near[...], preferred_element_type=F32).astype(BF)
    copies[1].wait()
    copies[2].wait()


def fetch(picks, din, dqkv, table):
    far = pl.BlockSpec(memory_space=pltpu.HBM)
    shapes = [din.shape, dqkv.shape, (picks.shape[0], table.shape[1])]
    big = [pltpu.with_memory_space_constraint(a, pltpu.HBM) for a in (din, dqkv, table)]
    return pl.pallas_call(
        fetch_kernel,
        out_shape=[pltpu.VMEM(s, BF) for s in shapes],
        in_specs=[VM, far, far, far],
        out_specs=[VM] * 3,
        scratch_shapes=[pltpu.VMEM(table.shape, BF), pltpu.SemaphoreType.DMA((3,))],
        compiler_params=pltpu.CompilerParams(vmem_limit_bytes=14 << 20),
    )(pltpu.with_memory_space_constraint(picks, pltpu.VMEM), *big)


def depth_first(ids, low, high, *rest):
    o_ref, z = rest[11:13]
    z[0:16, :] = low[...]
    z[128:144, :] = high[...]
    for i in range(3):
        at = (i + 1) * 16
        z[at:at + 16, :] = rest[i][0]
        z[128 + at:144 + at, :] = rest[i][1]
    for i in range(4):
        at = (i + 4) * 16
        z[at:at + 16, :] = rest[3 + i][...]
        z[128 + at:144 + at, :] = rest[7 + i][...]
    depth_rows(ids, z, 128, o_ref)


def depth_second(ids, z, o_ref):
    depth_rows(ids, z, 0, o_ref)


def depth_rows(ids, z, at, o_ref):
    section = ids[1]
    rows = at + lax.broadcasted_iota(jnp.int32, (128, 1), 0)
    cols = lax.broadcasted_iota(jnp.int32, (1, 256), 1)
    rpos = place(rows, section, 16) // 16
    cpos = place(cols, section, 16) // 16
    keep = (cpos <= rpos) & (rows % 16 == cols % 16)
    bias = jnp.where(keep, 0.0, NEG)
    low = lax.broadcasted_iota(jnp.int32, (128, 2 * DHEAD), 1) < DHEAD
    inner = z.shape[1] // 3
    for pair in range(inner // (2 * DHEAD)):
        base = pair * 2 * DHEAD
        q = z[at:at + 128, base:base + 2 * DHEAD]
        k = z[:, inner + base:inner + base + 2 * DHEAD]
        v = z[:, 2 * inner + base:2 * inner + base + 2 * DHEAD]
        got = []
        for side in range(2):
            mask = low if side == 0 else jnp.logical_not(low)
            qs = jnp.where(mask, q, jnp.zeros_like(q))
            s = lax.dot_general(
                qs, k, (((1,), (1,)), ((), ())), preferred_element_type=F32
            )
            s = s * (1.0 / math.sqrt(DHEAD)) + bias
            top = jnp.max(s, axis=-1, keepdims=True)
            e = jnp.exp(s - top)
            total = jnp.sum(e, axis=-1, keepdims=True)
            o = jnp.dot(e.astype(BF), v, preferred_element_type=F32)
            got.append(o / total)
        res = jnp.where(low, got[0], got[1]).astype(BF)
        o_ref[:, :, base:base + 2 * DHEAD] = res.reshape(8, 16, 2 * DHEAD)


def join_kernel(a_ref, b_ref, *outs):
    for e, o_ref in enumerate(outs):
        o_ref[0] = a_ref[e]
        o_ref[1] = b_ref[e]


def final_kernel(ids, *rest):
    o_ref = rest[8]
    for e in range(8):
        o_ref[ids[1] ^ (2 * e)] = rest[e][0]
        o_ref[ids[1] ^ (2 * e + 1)] = rest[e][1]


def add_kernel(*refs):
    part = refs[0][...].astype(F32)
    for ref in refs[1:-1]:
        part = part + ref[...].astype(F32)
    refs[-1][...] = part.astype(BF)


def add(*values):
    return call(add_kernel, [(values[0].shape, BF)], n_in=len(values), limit=2)(*values)[0]


def gather(value, across=False):
    def cb(v, flip):
        return swap(v, "cb", 16, flip)

    y = cb(value, 8)
    x1 = cb(value, 2)
    x3 = cb(value, 6)
    x2 = cb(value, 4)
    y1 = cb(y, 2)
    y3 = cb(y, 6)
    y2 = cb(y, 4) if across else cb(x2, 8)
    return [value, x1, x2, x3, y, y1, y2, y3]


def work(frames_in, valid_len, tokens, t_gain, w_qkv, w_out, h_gain, d_in, d_embed, d_gain, d_qkv):
    model = frames_in.shape[2]
    mine = frames_in[0]
    f = lax.axis_index("fsdp").astype(jnp.int32)
    c = lax.axis_index("cb").astype(jnp.int32)
    ids = jnp.stack([f, c, valid_len[0]])
    fs = lambda v, flip: swap(v, "fsdp", 8, flip)
    cb = lambda v, flip: swap(v, "cb", 16, flip)
    block = model // 8

    rel = call(norm_kernel, [((8, 16, block), BF)], smem=1, n_in=3)(
        ids, mine, t_gain[None]
    )[0]
    near = fs(w_out, 1)
    w_other = fs(w_qkv, 1)
    local = [rel[0:2]] + [fs(rel[2 * d:2 * d + 2], 2 * d) for d in (1, 2, 3)]
    local = jnp.concatenate(local, axis=0)
    wo_even = [w_out] + [fs(w_out, 2 * d) for d in (1, 2, 3)]
    wo_odd = [near] + [fs(near, 2 * d) for d in (1, 2, 3)]
    wo = [w for pair in zip(wo_even, wo_odd) for w in pair]
    even = jnp.stack(gather(local, True))
    odd = cb(even, 1)
    cols = w_qkv.shape[1]

    def project(src, kinds):
        return call(qkv_kernel, [((128, cols), k) for k in kinds], n_in=3)(
            src, w_qkv, w_other
        )

    a0, a1, a2, a3 = project(even, (F32, BF, BF, F32))
    relay_a = fs(a2, 2)
    plain_a = fs(a1, 2)
    b0, b1, b2, b3 = project(odd, (F32, F32, BF, BF))
    relay_b = fs(b2, 6)
    plain_b = fs(b3, 6)
    sum_a = fs(add(a3, relay_a), 6)
    sum_b = fs(add(b1, relay_b), 2)
    give, left = call(
        attn_kernel,
        [((128, model), BF), ((128, w_out.shape[0]), BF)],
        scratch=[pltpu.VMEM((256, cols), BF), pltpu.VMEM((256, w_out.shape[0]), BF)],
        smem=1,
        n_in=15,
    )(ids, a0, plain_a, sum_a, b0, plain_b, sum_b, *wo)
    taken = cb(give, 1)
    keep = call(keep_kernel, [((128, model), BF)], n_in=9)(left, *wo)[0]
    blocks = call(pair_kernel, [((16, model), F32)] + [((16, model), BF)] * 7, n_in=2)(
        keep, taken
    )
    far1, far3 = cb(blocks[5], 2), cb(blocks[7], 6)
    far2 = cb(blocks[6], 8)
    near1, near3 = cb(blocks[1], 2), cb(blocks[3], 6)
    side = add(blocks[4], far1, far3)
    deep = add(blocks[2], far2)
    pieces = [blocks[0], near1, near3, cb(side, 8), cb(deep, 4)]
    hn = call(
        hidden_kernel,
        [((16, model), BF)],
        scratch=[pltpu.VMEM((8, 16, block), F32)],
        smem=1,
        n_in=8,
    )(ids, mine, h_gain[None], *pieces)[0]
    even = jnp.stack(gather(hn))
    odd = cb(even, 1)

    order = jnp.concatenate([2 * jnp.arange(8), 2 * jnp.arange(8) + 1]).astype(jnp.int32)
    mine_at = (jnp.arange(16, dtype=jnp.int32)[None, :] == (c ^ order)[:, None])[:, :, None]
    picks = jnp.sum(jnp.where(mine_at, tokens[0, 0].reshape(1, 16, 16), 0), axis=1)
    din, dqkv, emb = fetch(picks.reshape(256, 1), d_in[0], d_qkv[0], d_embed[0])
    inner = d_in.shape[2]

    def lift(src, row, outs):
        return call(functools.partial(lift_kernel, row), outs, n_in=5, limit=12)(
            src, din, emb, d_gain, dqkv
        )

    low = lift(even, 0, [((16, 3 * inner), BF)] * 8)
    high = lift(odd, 128, [((8, 16, 3 * inner), BF)])[0]
    high = cb(high, 1)
    got = {e: cb(low[e], 2 * e) for e in (5, 7)}
    got.update({e: cb(low[e], 2 * e) for e in (6, 4)})
    both = [cb(jnp.stack([low[e], high[e]]), 2 * e) for e in (2, 1, 3)]
    deep = [cb(high[e], 2 * e) for e in (4, 5, 6, 7)]
    both = [both[1], both[0], both[2]]
    other, z = call(
        depth_first,
        [((8, 16, inner), BF), ((256, 3 * inner), BF)],
        smem=1,
        n_in=14,
    )(ids, low[0], high[0], *both, *[got[e] for e in (4, 5, 6, 7)], *deep)
    other = cb(other, 1)
    outs = call(depth_second, [((8, 16, inner), BF)], smem=1, n_in=2)(ids, z)[0]
    outs = call(join_kernel, [((2, 16, inner), BF)] * 8, n_in=2)(outs, other)
    pieces = [outs[0]] + [cb(outs[e], 2 * e) for e in range(1, 8)]
    out = call(final_kernel, [((16, 16, inner), BF)], smem=1, n_in=9, last=True)(
        ids, *pieces
    )[0]
    return out.reshape(1, 1, 256, inner)


def solution(mesh):
    placed = (
        P("fsdp", "cb", None),
        P("fsdp"),
        P("fsdp", "cb", None),
        P(),
        P("fsdp", "cb"),
        P("cb", "fsdp"),
        P(),
        P("cb", None, None),
        P("cb", None, None),
        P("cb", None),
        P("cb", None, None),
    )
    return jax.shard_map(
        work, mesh=mesh, in_specs=placed, out_specs=P("fsdp", "cb", None, None), check_vma=False
    )
```

```python
import functools
import math

import jax
import jax.numpy as jnp
from jax import lax
from jax.experimental import pallas as pl
from jax.experimental.pallas import tpu as pltpu
from jax.sharding import PartitionSpec as P


HEAD = 128
DHEAD = 64
EPS = 1e-05
NEG = -1e30
BF = jnp.bfloat16
F32 = jnp.float32


VM = pl.BlockSpec(memory_space=pltpu.VMEM)
SM = pl.BlockSpec(memory_space=pltpu.SMEM)


def swap(value, axis, size, flip):
    return lax.ppermute(value, axis, [(i, i ^ flip) for i in range(size)])


def call(kernel, outs, scratch=(), smem=0, n_in=0, limit=8):
    kind = pltpu.VMEM
    run = pl.pallas_call(
        kernel,
        out_shape=[kind(s, d) for s, d in outs],
        in_specs=[SM] * smem + [VM] * (n_in - smem),
        out_specs=[VM] * len(outs),
        scratch_shapes=list(scratch),
        compiler_params=pltpu.CompilerParams(vmem_limit_bytes=limit << 20),
    )

    def go(*args):
        held = [pltpu.with_memory_space_constraint(a, pltpu.VMEM) for a in args[smem:]]
        return run(*args[:smem], *held)

    return go


def norm_kernel(ids, x_ref, g_ref, o_ref):
    x = x_ref[...].astype(F32)
    scale = lax.rsqrt(jnp.mean(x * x, axis=-1, keepdims=True) + EPS)
    y = (x * scale * g_ref[...]).astype(BF)
    width = o_ref.shape[2]
    for b in range(o_ref.shape[0]):
        o_ref[ids[0] ^ b] = y[:, b * width:(b + 1) * width]


def qkv_kernel(src, wa, wb, va, vb, *outs):
    half = wa.shape[0]
    for d, o_ref in enumerate(outs):
        acc = None
        for h, pair in enumerate(((wa, wb), (va, vb))):
            rows = src[:, 2 * d + h].reshape(-1, 2 * half)
            for i, w in enumerate(pair):
                part = jnp.dot(
                    rows[:, i * half:(i + 1) * half], w[...], preferred_element_type=F32
                )
                acc = part if acc is None else acc + part
        o_ref[...] = acc.astype(o_ref.dtype)


def cut_kernel(src, *rest):
    outs, sems = rest[:-1], rest[-1]
    rows = outs[0].shape[0]
    copies = [
        pltpu.make_async_copy(src.at[pl.ds(i * rows, rows)], o, sems.at[i])
        for i, o in enumerate(outs)
    ]
    for copy in copies:
        copy.start()
    for copy in copies:
        copy.wait()


def cut(value):
    half = (value.shape[0] // 2, value.shape[1])
    return pl.pallas_call(
        cut_kernel,
        out_shape=[pltpu.VMEM(half, value.dtype)] * 2,
        in_specs=[pl.BlockSpec(memory_space=pltpu.HBM)],
        out_specs=[VM] * 2,
        scratch_shapes=[pltpu.SemaphoreType.DMA((2,))],
        compiler_params=pltpu.CompilerParams(vmem_limit_bytes=1 << 20),
    )(pltpu.with_memory_space_constraint(value, pltpu.HBM))


def place(row, section, step):
    group = row // step
    half = group // 8
    return (section ^ (2 * (group - 8 * half) + half)) * step + (row - group * step)


def attn_kernel(ids, a0, a1, a2, b0, b1, b2, *rest):
    wo = rest[:8]
    give, left = rest[8:10]
    packed = rest[10]
    mixed = rest[11]
    length, width = packed.shape
    half = length // 2
    for at, trio in ((0, (a0, a1, a2)), (half, (b0, b1, b2))):
        part = trio[0][...] + trio[1][...].astype(F32) + trio[2][...].astype(F32)
        packed[at:at + half, :] = part.astype(BF)
    section = ids[1]
    valid = ids[2]
    rows = place(lax.broadcasted_iota(jnp.int32, (length, 1), 0), section, 16)
    cols = place(lax.broadcasted_iota(jnp.int32, (1, length), 1), section, 16)
    allowed = (cols <= rows) & (cols < valid)
    for h in range(width // (3 * HEAD)):
        base = h * 3 * HEAD
        q = packed[:, base:base + HEAD]
        k = packed[:, base + HEAD:base + 2 * HEAD]
        v = packed[:, base + 2 * HEAD:base + 3 * HEAD]
        s = lax.dot_general(q, k, (((1,), (1,)), ((), ())), preferred_element_type=F32)
        s = jnp.where(allowed, s * (1.0 / math.sqrt(HEAD)), NEG)
        top = jnp.max(s, axis=-1, keepdims=True)
        e = jnp.where(allowed, jnp.exp(s - top), 0.0)
        p = (e / jnp.sum(e, axis=-1, keepdims=True)).astype(BF)
        mixed[:, h * HEAD:(h + 1) * HEAD] = jnp.dot(
            p, v, preferred_element_type=F32
        ).astype(BF)
    left[...] = mixed[:half, :]
    spread(mixed[half:, :], wo, give)


def spread(rows, wo, o_ref):
    width = wo[0].shape[1]
    for e in range(8):
        acc = jnp.dot(rows, wo[e][...], preferred_element_type=F32)
        o_ref[:, e * width:(e + 1) * width] = acc.astype(BF)


def keep_kernel(left, *rest):
    spread(left[...], rest[:8], rest[8])


def pair_kernel(a_ref, b_ref, *outs):
    for j, o_ref in enumerate(outs):
        rows = o_ref.shape[0]
        part = a_ref[j * rows:(j + 1) * rows, :].astype(F32) + b_ref[
            j * rows:(j + 1) * rows, :
        ].astype(F32)
        o_ref[...] = part.astype(o_ref.dtype)


def hidden_kernel(ids, frames, gain, *rest):
    pieces = rest[:5]
    o_ref = rest[5]
    acc = rest[6]
    width = frames.shape[1] // 8
    for e in range(8):
        cut = slice(e * width, (e + 1) * width)
        part = pieces[0][:, cut].astype(F32)
        for piece in pieces[1:]:
            part = part + piece[:, cut].astype(F32)
        acc[ids[0] ^ e] = part
    total = jnp.zeros((frames.shape[0], 1), F32)
    for b in range(8):
        cut = slice(b * width, (b + 1) * width)
        hid = frames[:, cut].astype(F32) + acc[b]
        acc[b] = hid
        total = total + jnp.sum(hid * hid, axis=-1, keepdims=True)
    scale = lax.rsqrt(total / frames.shape[1] + EPS)
    for b in range(8):
        cut = slice(b * width, (b + 1) * width)
        o_ref[:, cut] = (acc[b] * scale * gain[:, cut]).astype(BF)


def lift_kernel(row, src, din, emb, gain, wqkv, *outs):
    x = src[...].reshape(-1, src.shape[2])
    near = emb[row:row + 8].reshape(x.shape[0], -1).astype(F32)
    lifted = jnp.dot(x, din[...], preferred_element_type=F32) + near
    scale = lax.rsqrt(jnp.mean(lifted * lifted, axis=-1, keepdims=True) + EPS)
    dn = (lifted * scale * gain[...]).astype(BF)
    step = 1024
    for s in range(wqkv.shape[1] // step):
        cut = slice(s * step, (s + 1) * step)
        y = jnp.dot(dn, wqkv[:, cut], preferred_element_type=F32).astype(BF)
        for e in range(8):
            if len(outs) == 8:
                outs[e][:, cut] = y[e * 16:(e + 1) * 16]
            else:
                outs[0][e, :, cut] = y[e * 16:(e + 1) * 16]


def load_kernel(src, dst, sem):
    copy = pltpu.make_async_copy(src, dst, sem)
    copy.start()
    copy.wait()


def load(value):
    return pl.pallas_call(
        load_kernel,
        out_shape=pltpu.VMEM(value.shape, value.dtype),
        in_specs=[pl.BlockSpec(memory_space=pltpu.HBM)],
        out_specs=VM,
        scratch_shapes=[pltpu.SemaphoreType.DMA],
        compiler_params=pltpu.CompilerParams(vmem_limit_bytes=1 << 20),
    )(pltpu.with_memory_space_constraint(value, pltpu.HBM))


def fetch_kernel(ids, picks, dqkv, table, dqkv_o, rows_o, near, sems):
    moves = ((table, near), (dqkv, dqkv_o))
    copies = [
        pltpu.make_async_copy(src, dst, sems.at[i]) for i, (src, dst) in enumerate(moves)
    ]
    for copy in copies:
        copy.start()
    count = near.shape[0]
    entry = lax.broadcasted_iota(jnp.int32, (count, picks.shape[1]), 0)
    hot = jnp.where(entry == picks[...], 1.0, 0.0).astype(BF)
    copies[0].wait()
    rows = lax.dot_general(
        hot, near[...], (((0,), (0,)), ((), ())), preferred_element_type=F32
    ).astype(BF)
    step = rows_o.shape[1]
    for b in range(rows_o.shape[0]):
        flip = ids[1] ^ b
        rows_o[8 * (flip % 2) + flip // 2] = rows[b * step:(b + 1) * step]
    copies[1].wait()


def fetch(ids, picks, dqkv, table):
    far = pl.BlockSpec(memory_space=pltpu.HBM)
    shapes = [dqkv.shape, (16, picks.shape[1] // 16, table.shape[1])]
    big = [pltpu.with_memory_space_constraint(a, pltpu.HBM) for a in (dqkv, table)]
    return pl.pallas_call(
        fetch_kernel,
        out_shape=[pltpu.VMEM(s, BF) for s in shapes],
        in_specs=[SM, VM, far, far],
        out_specs=[VM] * 2,
        scratch_shapes=[pltpu.VMEM(table.shape, BF), pltpu.SemaphoreType.DMA((2,))],
        compiler_params=pltpu.CompilerParams(vmem_limit_bytes=14 << 20),
    )(ids, pltpu.with_memory_space_constraint(picks, pltpu.VMEM), *big)


def depth_kernel(ids, low, high, *rest):
    o_ref, z = rest[11:13]
    z[0:16, :] = low[...]
    z[128:144, :] = high[...]
    for i in range(3):
        at = (i + 1) * 16
        z[at:at + 16, :] = rest[i][0]
        z[128 + at:144 + at, :] = rest[i][1]
    for i in range(4):
        at = (i + 4) * 16
        z[at:at + 16, :] = rest[3 + i][...]
        z[128 + at:144 + at, :] = rest[7 + i][...]
    section = ids[1]
    rows = lax.broadcasted_iota(jnp.int32, (256, 1), 0)
    cols = lax.broadcasted_iota(jnp.int32, (1, 256), 1)
    rpos = place(rows, section, 16) // 16
    cpos = place(cols, section, 16) // 16
    keep = (cpos <= rpos) & (rows % 16 == cols % 16)
    bias = jnp.where(keep, 0.0, NEG)
    first = lax.broadcasted_iota(jnp.int32, (256, 2 * DHEAD), 1) < DHEAD
    inner = z.shape[1] // 3
    for pair in range(inner // (2 * DHEAD)):
        base = pair * 2 * DHEAD
        q = z[:, base:base + 2 * DHEAD]
        k = z[:, inner + base:inner + base + 2 * DHEAD]
        v = z[:, 2 * inner + base:2 * inner + base + 2 * DHEAD]
        got = []
        for side in range(2):
            mask = first if side == 0 else jnp.logical_not(first)
            qs = jnp.where(mask, q, jnp.zeros_like(q))
            s = lax.dot_general(
                qs, k, (((1,), (1,)), ((), ())), preferred_element_type=F32
            )
            s = s * (1.0 / math.sqrt(DHEAD)) + bias
            top = jnp.max(s, axis=-1, keepdims=True)
            e = jnp.exp(s - top)
            total = jnp.sum(e, axis=-1, keepdims=True)
            o = jnp.dot(e.astype(BF), v, preferred_element_type=F32)
            got.append(o / total)
        res = jnp.where(first, got[0], got[1]).astype(BF)
        for m in range(16):
            to = section ^ (2 * (m % 8) + m // 8)
            o_ref[to, :, base:base + 2 * DHEAD] = res[m * 16:(m + 1) * 16]


def add_kernel(*refs):
    part = refs[0][...].astype(F32)
    for ref in refs[1:-1]:
        part = part + ref[...].astype(F32)
    refs[-1][...] = part.astype(BF)


def add(*values):
    return call(add_kernel, [(values[0].shape, BF)], n_in=len(values), limit=2)(*values)[0]


def gather(value, across=False):
    def cb(v, flip):
        return swap(v, "cb", 16, flip)

    y = cb(value, 8)
    x1 = cb(value, 2)
    x3 = cb(value, 6)
    x2 = cb(value, 4)
    y1 = cb(y, 2)
    y3 = cb(y, 6)
    y2 = cb(y, 4) if across else cb(x2, 8)
    return [value, x1, x2, x3, y, y1, y2, y3]


def work(frames_in, valid_len, tokens, t_gain, w_qkv, w_out, h_gain, d_in, d_embed, d_gain, d_qkv):
    model = frames_in.shape[2]
    mine = frames_in[0]
    f = lax.axis_index("fsdp").astype(jnp.int32)
    c = lax.axis_index("cb").astype(jnp.int32)
    ids = jnp.stack([f, c, valid_len[0]])
    fs = lambda v, flip: swap(v, "fsdp", 8, flip)
    cb = lambda v, flip: swap(v, "cb", 16, flip)
    block = model // 8

    rel = call(norm_kernel, [((8, 16, block), BF)], smem=1, n_in=3)(
        ids, mine, t_gain[None]
    )[0]
    near = fs(w_out, 1)
    wa, wb = cut(w_qkv)
    va = fs(wa, 1)
    vb = fs(wb, 1)
    local = [rel[0:2]] + [fs(rel[2 * d:2 * d + 2], 2 * d) for d in (1, 2, 3)]
    local = jnp.concatenate(local, axis=0)
    wo_even = [w_out] + [fs(w_out, 2 * d) for d in (1, 2, 3)]
    odd1, odd3 = fs(near, 2), fs(near, 6)
    odd2 = fs(wo_even[2], 1)
    wo_odd = [near, odd1, odd2, odd3]
    wo = [w for pair in zip(wo_even, wo_odd) for w in pair]
    even = jnp.stack(gather(local, True))
    odd = cb(even, 1)
    cols = w_qkv.shape[1]

    def project(src, kinds):
        return call(qkv_kernel, [((128, cols), k) for k in kinds], n_in=5)(
            src, wa, wb, va, vb
        )

    a0, a1, a2, a3 = project(even, (F32, BF, BF, F32))
    relay_a = fs(a2, 2)
    plain_a = fs(a1, 2)
    b0, b1, b2, b3 = project(odd, (F32, F32, BF, BF))
    relay_b = fs(b2, 6)
    plain_b = fs(b3, 6)
    sum_a = fs(add(a3, relay_a), 6)
    sum_b = fs(add(b1, relay_b), 2)
    give, left = call(
        attn_kernel,
        [((128, model), BF), ((128, w_out.shape[0]), BF)],
        scratch=[pltpu.VMEM((256, cols), BF), pltpu.VMEM((256, w_out.shape[0]), BF)],
        smem=1,
        n_in=15,
    )(ids, a0, plain_a, sum_a, b0, plain_b, sum_b, *wo)
    taken = cb(give, 1)
    keep = call(keep_kernel, [((128, model), BF)], n_in=9)(left, *wo)[0]
    blocks = call(pair_kernel, [((16, model), F32)] + [((16, model), BF)] * 7, n_in=2)(
        keep, taken
    )
    far1, far3 = cb(blocks[5], 2), cb(blocks[7], 6)
    far2 = cb(blocks[6], 8)
    near1, near3 = cb(blocks[1], 2), cb(blocks[3], 6)
    side = add(blocks[4], far1, far3)
    deep = add(blocks[2], far2)
    pieces = [blocks[0], near1, near3, cb(side, 8), cb(deep, 4)]
    hn = call(
        hidden_kernel,
        [((16, model), BF)],
        scratch=[pltpu.VMEM((8, 16, block), F32)],
        smem=1,
        n_in=8,
    )(ids, mine, h_gain[None], *pieces)[0]
    even = jnp.stack(gather(hn))
    odd = cb(even, 1)

    din = load(d_in[0])
    dqkv, emb = fetch(ids, tokens[0], d_qkv[0], d_embed[0])
    inner = d_in.shape[2]

    def lift(src, row, outs):
        return call(functools.partial(lift_kernel, row), outs, n_in=5, limit=12)(
            src, din, emb, d_gain, dqkv
        )

    low = lift(even, 0, [((16, 3 * inner), BF)] * 8)
    high = lift(odd, 8, [((8, 16, 3 * inner), BF)])[0]
    high = cb(high, 1)
    got = {e: cb(low[e], 2 * e) for e in (5, 7)}
    got.update({e: cb(low[e], 2 * e) for e in (6, 4)})
    both = [cb(jnp.stack([low[e], high[e]]), 2 * e) for e in (2, 1, 3)]
    deep = [cb(high[e], 2 * e) for e in (4, 5, 6, 7)]
    both = [both[1], both[0], both[2]]
    outs = call(
        depth_kernel,
        [((16, 16, inner), BF)],
        scratch=[pltpu.VMEM((256, 3 * inner), BF)],
        smem=1,
        n_in=14,
    )(ids, low[0], high[0], *both, *[got[e] for e in (4, 5, 6, 7)], *deep)[0]
    out = lax.all_to_all(outs, "cb", 0, 0, tiled=True)
    return out.reshape(1, 1, 256, inner)


def solution(mesh):
    placed = (
        P("fsdp", "cb", None),
        P("fsdp"),
        P("fsdp", "cb", None),
        P(),
        P("fsdp", "cb"),
        P("cb", "fsdp"),
        P(),
        P("cb", None, None),
        P("cb", None, None),
        P("cb", None),
        P("cb", None, None),
    )
    return jax.shard_map(
        work, mesh=mesh, in_specs=placed, out_specs=P("fsdp", "cb", None, None), check_vma=False
    )
```

```python
import functools
import math

import jax
import jax.numpy as jnp
from jax import lax
from jax.experimental import pallas as pl
from jax.experimental.pallas import tpu as pltpu
from jax.sharding import PartitionSpec as P


HEAD = 128
DHEAD = 64
EPS = 1e-05
NEG = -1e30
BF = jnp.bfloat16
F32 = jnp.float32


SENDS = (
    ("l", 6), ("l", 7), ("l", 5), ("b", 2), ("h", 6), ("b", 3), ("h", 7), ("b", 1),
    ("h", 5), ("l", 4), ("h", 4),
)

VM = pl.BlockSpec(memory_space=pltpu.VMEM)
SM = pl.BlockSpec(memory_space=pltpu.SMEM)


def swap(value, axis, size, flip):
    return lax.ppermute(value, axis, [(i, i ^ flip) for i in range(size)])


def call(kernel, outs, scratch=(), smem=0, n_in=0, limit=8):
    kind = pltpu.VMEM
    run = pl.pallas_call(
        kernel,
        out_shape=[kind(s, d) for s, d in outs],
        in_specs=[SM] * smem + [VM] * (n_in - smem),
        out_specs=[VM] * len(outs),
        scratch_shapes=list(scratch),
        compiler_params=pltpu.CompilerParams(vmem_limit_bytes=limit << 20),
    )

    def go(*args):
        held = [pltpu.with_memory_space_constraint(a, pltpu.VMEM) for a in args[smem:]]
        return run(*args[:smem], *held)

    return go


def first_kernel(ids, x_hbm, g_hbm, w_hbm, o_ref, wa, wb, x_ref, g_ref, sems):
    half = wa.shape[0]
    moves = (
        (x_hbm, x_ref),
        (g_hbm, g_ref),
        (w_hbm.at[pl.ds(0, half)], wa),
        (w_hbm.at[pl.ds(half, half)], wb),
    )
    copies = [
        pltpu.make_async_copy(src, dst, sems.at[i]) for i, (src, dst) in enumerate(moves)
    ]
    for copy in copies:
        copy.start()
    copies[0].wait()
    copies[1].wait()
    x = x_ref[...].astype(F32)
    scale = lax.rsqrt(jnp.mean(x * x, axis=-1, keepdims=True) + EPS)
    y = (x * scale * g_ref[...]).astype(BF)
    width = o_ref.shape[2]
    for b in range(o_ref.shape[0]):
        o_ref[ids[0] ^ b] = y[:, b * width:(b + 1) * width]
    copies[2].wait()
    copies[3].wait()


def first(ids, mine, gain, weight):
    far = pl.BlockSpec(memory_space=pltpu.HBM)
    half = (weight.shape[0] // 2, weight.shape[1])
    rel = (8, mine.shape[0], mine.shape[1] // 8)
    big = [pltpu.with_memory_space_constraint(a, pltpu.HBM) for a in (mine, gain, weight)]
    return pl.pallas_call(
        first_kernel,
        out_shape=[pltpu.VMEM(s, BF) for s in (rel, half, half)],
        in_specs=[SM, far, far, far],
        out_specs=[VM] * 3,
        scratch_shapes=[
            pltpu.VMEM(mine.shape, BF),
            pltpu.VMEM(gain.shape, F32),
            pltpu.SemaphoreType.DMA((4,)),
        ],
        compiler_params=pltpu.CompilerParams(vmem_limit_bytes=8 << 20),
    )(ids, *big)


def qkv_kernel(src, wa, wb, va, vb, *outs):
    half = wa.shape[0]
    for d, o_ref in enumerate(outs):
        acc = None
        for h, pair in enumerate(((wa, wb), (va, vb))):
            rows = src[:, 2 * d + h].reshape(-1, 2 * half)
            for i, w in enumerate(pair):
                part = jnp.dot(
                    rows[:, i * half:(i + 1) * half], w[...], preferred_element_type=F32
                )
                acc = part if acc is None else acc + part
        o_ref[...] = acc.astype(o_ref.dtype)


def place(row, section, step):
    group = row // step
    half = group // 8
    return (section ^ (2 * (group - 8 * half) + half)) * step + (row - group * step)


def attn_kernel(ids, a0, a1, a2, b0, b1, b2, *rest):
    wo = rest[:8]
    give, left = rest[8:10]
    packed = rest[10]
    mixed = rest[11]
    length, width = packed.shape
    half = length // 2
    for at, trio in ((0, (a0, a1, a2)), (half, (b0, b1, b2))):
        part = trio[0][...] + trio[1][...].astype(F32) + trio[2][...].astype(F32)
        packed[at:at + half, :] = part.astype(BF)
    section = ids[1]
    valid = ids[2]
    rows = place(lax.broadcasted_iota(jnp.int32, (length, 1), 0), section, 16)
    cols = place(lax.broadcasted_iota(jnp.int32, (1, length), 1), section, 16)
    allowed = (cols <= rows) & (cols < valid)
    for h in range(width // (3 * HEAD)):
        base = h * 3 * HEAD
        q = packed[:, base:base + HEAD]
        k = packed[:, base + HEAD:base + 2 * HEAD]
        v = packed[:, base + 2 * HEAD:base + 3 * HEAD]
        s = lax.dot_general(q, k, (((1,), (1,)), ((), ())), preferred_element_type=F32)
        s = jnp.where(allowed, s * (1.0 / math.sqrt(HEAD)), NEG)
        top = jnp.max(s, axis=-1, keepdims=True)
        e = jnp.where(allowed, jnp.exp(s - top), 0.0)
        p = (e / jnp.sum(e, axis=-1, keepdims=True)).astype(BF)
        mixed[:, h * HEAD:(h + 1) * HEAD] = jnp.dot(
            p, v, preferred_element_type=F32
        ).astype(BF)
    left[...] = mixed[:half, :]
    spread(mixed[half:, :], wo, give)


def spread(rows, wo, o_ref):
    width = wo[0].shape[1]
    for e in range(8):
        acc = jnp.dot(rows, wo[e][...], preferred_element_type=F32)
        o_ref[:, e * width:(e + 1) * width] = acc.astype(BF)


def keep_kernel(left, *rest):
    spread(left[...], rest[:8], rest[8])


def pair_kernel(a_ref, b_ref, *outs):
    for j, o_ref in enumerate(outs):
        rows = o_ref.shape[0]
        part = a_ref[j * rows:(j + 1) * rows, :].astype(F32) + b_ref[
            j * rows:(j + 1) * rows, :
        ].astype(F32)
        o_ref[...] = part.astype(o_ref.dtype)


def hidden_kernel(ids, frames, gain, *rest):
    pieces = rest[:5]
    o_ref = rest[5]
    acc = rest[6]
    width = frames.shape[1] // 8
    for e in range(8):
        cut = slice(e * width, (e + 1) * width)
        part = pieces[0][:, cut].astype(F32)
        for piece in pieces[1:]:
            part = part + piece[:, cut].astype(F32)
        acc[ids[0] ^ e] = part
    total = jnp.zeros((frames.shape[0], 1), F32)
    for b in range(8):
        cut = slice(b * width, (b + 1) * width)
        hid = frames[:, cut].astype(F32) + acc[b]
        acc[b] = hid
        total = total + jnp.sum(hid * hid, axis=-1, keepdims=True)
    scale = lax.rsqrt(total / frames.shape[1] + EPS)
    for b in range(8):
        cut = slice(b * width, (b + 1) * width)
        o_ref[:, cut] = (acc[b] * scale * gain[:, cut]).astype(BF)


def lift_kernel(row, src, din, emb, gain, wqkv, *outs):
    x = src[...].reshape(-1, src.shape[2])
    near = emb[row:row + 8].reshape(x.shape[0], -1).astype(F32)
    lifted = jnp.dot(x, din[...], preferred_element_type=F32) + near
    scale = lax.rsqrt(jnp.mean(lifted * lifted, axis=-1, keepdims=True) + EPS)
    dn = (lifted * scale * gain[...]).astype(BF)
    step = 1024
    for s in range(wqkv.shape[1] // step):
        cut = slice(s * step, (s + 1) * step)
        y = jnp.dot(dn, wqkv[:, cut], preferred_element_type=F32).astype(BF)
        for e in range(8):
            if len(outs) == 8:
                outs[e][:, cut] = y[e * 16:(e + 1) * 16]
            else:
                outs[0][e, :, cut] = y[e * 16:(e + 1) * 16]


def load_kernel(src, dst, sem):
    copy = pltpu.make_async_copy(src, dst, sem)
    copy.start()
    copy.wait()


def load(value):
    return pl.pallas_call(
        load_kernel,
        out_shape=pltpu.VMEM(value.shape, value.dtype),
        in_specs=[pl.BlockSpec(memory_space=pltpu.HBM)],
        out_specs=VM,
        scratch_shapes=[pltpu.SemaphoreType.DMA],
        compiler_params=pltpu.CompilerParams(vmem_limit_bytes=1 << 20),
    )(pltpu.with_memory_space_constraint(value, pltpu.HBM))


def fetch_kernel(ids, picks, dqkv, table, dqkv_o, rows_o, near, sems):
    moves = ((table, near), (dqkv, dqkv_o))
    copies = [
        pltpu.make_async_copy(src, dst, sems.at[i]) for i, (src, dst) in enumerate(moves)
    ]
    for copy in copies:
        copy.start()
    count = near.shape[0]
    entry = lax.broadcasted_iota(jnp.int32, (count, picks.shape[1]), 0)
    hot = jnp.where(entry == picks[...], 1.0, 0.0).astype(BF)
    copies[0].wait()
    rows = lax.dot_general(
        hot, near[...], (((0,), (0,)), ((), ())), preferred_element_type=F32
    ).astype(BF)
    step = rows_o.shape[1]
    for b in range(rows_o.shape[0]):
        flip = ids[1] ^ b
        rows_o[8 * (flip % 2) + flip // 2] = rows[b * step:(b + 1) * step]
    copies[1].wait()


def fetch(ids, picks, dqkv, table):
    far = pl.BlockSpec(memory_space=pltpu.HBM)
    shapes = [dqkv.shape, (16, picks.shape[1] // 16, table.shape[1])]
    big = [pltpu.with_memory_space_constraint(a, pltpu.HBM) for a in (dqkv, table)]
    return pl.pallas_call(
        fetch_kernel,
        out_shape=[pltpu.VMEM(s, BF) for s in shapes],
        in_specs=[SM, VM, far, far],
        out_specs=[VM] * 2,
        scratch_shapes=[pltpu.VMEM(table.shape, BF), pltpu.SemaphoreType.DMA((2,))],
        compiler_params=pltpu.CompilerParams(vmem_limit_bytes=14 << 20),
    )(ids, pltpu.with_memory_space_constraint(picks, pltpu.VMEM), *big)


def depth_kernel(ids, low, high, *rest):
    o_ref, z = rest[11:13]
    z[0:16, :] = low[...]
    z[128:144, :] = high[...]
    for i in range(3):
        at = (i + 1) * 16
        z[at:at + 16, :] = rest[i][0]
        z[128 + at:144 + at, :] = rest[i][1]
    for i in range(4):
        at = (i + 4) * 16
        z[at:at + 16, :] = rest[3 + i][...]
        z[128 + at:144 + at, :] = rest[7 + i][...]
    section = ids[1]
    rows = lax.broadcasted_iota(jnp.int32, (256, 1), 0)
    cols = lax.broadcasted_iota(jnp.int32, (1, 256), 1)
    rpos = place(rows, section, 16) // 16
    cpos = place(cols, section, 16) // 16
    keep = (cpos <= rpos) & (rows % 16 == cols % 16)
    bias = jnp.where(keep, 0.0, NEG)
    first = lax.broadcasted_iota(jnp.int32, (256, 2 * DHEAD), 1) < DHEAD
    inner = z.shape[1] // 3
    for pair in range(inner // (2 * DHEAD)):
        base = pair * 2 * DHEAD
        q = z[:, base:base + 2 * DHEAD]
        k = z[:, inner + base:inner + base + 2 * DHEAD]
        v = z[:, 2 * inner + base:2 * inner + base + 2 * DHEAD]
        got = []
        for side in range(2):
            mask = first if side == 0 else jnp.logical_not(first)
            qs = jnp.where(mask, q, jnp.zeros_like(q))
            s = lax.dot_general(
                qs, k, (((1,), (1,)), ((), ())), preferred_element_type=F32
            )
            s = s * (1.0 / math.sqrt(DHEAD)) + bias
            top = jnp.max(s, axis=-1, keepdims=True)
            e = jnp.exp(s - top)
            total = jnp.sum(e, axis=-1, keepdims=True)
            o = jnp.dot(e.astype(BF), v, preferred_element_type=F32)
            got.append(o / total)
        res = jnp.where(first, got[0], got[1]).astype(BF)
        for m in range(16):
            to = section ^ (2 * (m % 8) + m // 8)
            o_ref[to, :, base:base + 2 * DHEAD] = res[m * 16:(m + 1) * 16]


def add_kernel(*refs):
    part = refs[0][...].astype(F32)
    for ref in refs[1:-1]:
        part = part + ref[...].astype(F32)
    refs[-1][...] = part.astype(BF)


def add(*values):
    return call(add_kernel, [(values[0].shape, BF)], n_in=len(values), limit=2)(*values)[0]


def gather(value, across=False):
    def cb(v, flip):
        return swap(v, "cb", 16, flip)

    y = cb(value, 8)
    x1 = cb(value, 2)
    x3 = cb(value, 6)
    x2 = cb(value, 4)
    y1 = cb(y, 2)
    y3 = cb(y, 6)
    y2 = cb(y, 4) if across else cb(x2, 8)
    return [value, x1, x2, x3, y, y1, y2, y3]


def work(frames_in, valid_len, tokens, t_gain, w_qkv, w_out, h_gain, d_in, d_embed, d_gain, d_qkv):
    model = frames_in.shape[2]
    mine = frames_in[0]
    f = lax.axis_index("fsdp").astype(jnp.int32)
    c = lax.axis_index("cb").astype(jnp.int32)
    ids = jnp.stack([f, c, valid_len[0]])
    fs = lambda v, flip: swap(v, "fsdp", 8, flip)
    cb = lambda v, flip: swap(v, "cb", 16, flip)
    block = model // 8

    rel, wa, wb = first(ids, mine, t_gain[None], w_qkv)
    near = fs(w_out, 1)
    va = fs(wa, 1)
    vb = fs(wb, 1)
    local = [rel[0:2]] + [fs(rel[2 * d:2 * d + 2], 2 * d) for d in (1, 2, 3)]
    local = jnp.concatenate(local, axis=0)
    wo_even = [w_out] + [fs(w_out, 2 * d) for d in (1, 2, 3)]
    odd1, odd3 = fs(near, 2), fs(near, 6)
    odd2 = fs(wo_even[2], 1)
    wo_odd = [near, odd1, odd2, odd3]
    wo = [w for pair in zip(wo_even, wo_odd) for w in pair]
    even = jnp.stack(gather(local, True))
    odd = cb(even, 1)
    cols = w_qkv.shape[1]

    def project(src, kinds):
        return call(qkv_kernel, [((128, cols), k) for k in kinds], n_in=5)(
            src, wa, wb, va, vb
        )

    a0, a1, a2, a3 = project(even, (F32, BF, BF, F32))
    relay_a = fs(a2, 2)
    plain_a = fs(a1, 2)
    b0, b1, b2, b3 = project(odd, (F32, F32, BF, BF))
    relay_b = fs(b2, 6)
    plain_b = fs(b3, 6)
    sum_a = fs(add(a3, relay_a), 6)
    sum_b = fs(add(b1, relay_b), 2)
    give, left = call(
        attn_kernel,
        [((128, model), BF), ((128, w_out.shape[0]), BF)],
        scratch=[pltpu.VMEM((256, cols), BF), pltpu.VMEM((256, w_out.shape[0]), BF)],
        smem=1,
        n_in=15,
    )(ids, a0, plain_a, sum_a, b0, plain_b, sum_b, *wo)
    taken = cb(give, 1)
    keep = call(keep_kernel, [((128, model), BF)], n_in=9)(left, *wo)[0]
    blocks = call(pair_kernel, [((16, model), F32)] + [((16, model), BF)] * 7, n_in=2)(
        keep, taken
    )
    far1, far3 = cb(blocks[5], 2), cb(blocks[7], 6)
    far2 = cb(blocks[6], 8)
    near1, near3 = cb(blocks[1], 2), cb(blocks[3], 6)
    side = add(blocks[4], far1, far3)
    deep = add(blocks[2], far2)
    last2 = cb(deep, 4)
    last1 = cb(side, 8)
    pieces = [blocks[0], near1, near3, last1, last2]
    hn = call(
        hidden_kernel,
        [((16, model), BF)],
        scratch=[pltpu.VMEM((8, 16, block), F32)],
        smem=1,
        n_in=8,
    )(ids, mine, h_gain[None], *pieces)[0]
    even = jnp.stack(gather(hn))
    odd = cb(even, 1)

    din = load(d_in[0])
    dqkv, emb = fetch(ids, tokens[0], d_qkv[0], d_embed[0])
    inner = d_in.shape[2]

    def lift(src, row, outs):
        return call(functools.partial(lift_kernel, row), outs, n_in=5, limit=12)(
            src, din, emb, d_gain, dqkv
        )

    low = lift(even, 0, [((16, 3 * inner), BF)] * 8)
    high = lift(odd, 8, [((8, 16, 3 * inner), BF)])[0]
    high = cb(high, 1)
    sent = {}
    for kind, e in SENDS:
        piece = {"l": low[e], "h": high[e]}.get(kind)
        if piece is None:
            piece = jnp.stack([low[e], high[e]])
        sent[kind, e] = cb(piece, 2 * e)
    both = [sent["b", e] for e in (1, 2, 3)]
    got = [sent["l", e] for e in (4, 5, 6, 7)]
    deep = [sent["h", e] for e in (4, 5, 6, 7)]
    outs = call(
        depth_kernel,
        [((16, 16, inner), BF)],
        scratch=[pltpu.VMEM((256, 3 * inner), BF)],
        smem=1,
        n_in=14,
    )(ids, low[0], high[0], *both, *got, *deep)[0]
    out = lax.all_to_all(outs, "cb", 0, 0, tiled=True)
    return out.reshape(1, 1, 256, inner)


def solution(mesh):
    placed = (
        P("fsdp", "cb", None),
        P("fsdp"),
        P("fsdp", "cb", None),
        P(),
        P("fsdp", "cb"),
        P("cb", "fsdp"),
        P(),
        P("cb", None, None),
        P("cb", None, None),
        P("cb", None),
        P("cb", None, None),
    )
    return jax.shard_map(
        work, mesh=mesh, in_specs=placed, out_specs=P("fsdp", "cb", None, None), check_vma=False
    )
```

```python
import functools
import math

import jax
import jax.numpy as jnp
from jax import lax
from jax.experimental import pallas as pl
from jax.experimental.pallas import tpu as pltpu
from jax.sharding import PartitionSpec as P


HEAD = 128
DHEAD = 64
EPS = 1e-05
NEG = -1e30
BF = jnp.bfloat16
F32 = jnp.float32


SENDS = (
    ("l", 7), ("l", 6), ("l", 5), ("b", 3), ("h", 7), ("b", 2), ("h", 6), ("b", 1),
    ("h", 5), ("l", 4), ("h", 4),
)

VM = pl.BlockSpec(memory_space=pltpu.VMEM)
SM = pl.BlockSpec(memory_space=pltpu.SMEM)


def swap(value, axis, size, flip):
    return lax.ppermute(value, axis, [(i, i ^ flip) for i in range(size)])


def call(kernel, outs, scratch=(), smem=0, n_in=0, limit=8):
    kind = pltpu.VMEM
    run = pl.pallas_call(
        kernel,
        out_shape=[kind(s, d) for s, d in outs],
        in_specs=[SM] * smem + [VM] * (n_in - smem),
        out_specs=[VM] * len(outs),
        scratch_shapes=list(scratch),
        compiler_params=pltpu.CompilerParams(vmem_limit_bytes=limit << 20),
    )

    def go(*args):
        held = [pltpu.with_memory_space_constraint(a, pltpu.VMEM) for a in args[smem:]]
        return run(*args[:smem], *held)

    return go


def first_kernel(ids, x_hbm, g_hbm, w_hbm, o_ref, wa, wb, x_ref, g_ref, sems):
    half = wa.shape[0]
    moves = (
        (x_hbm, x_ref),
        (g_hbm, g_ref),
        (w_hbm.at[pl.ds(0, half)], wa),
        (w_hbm.at[pl.ds(half, half)], wb),
    )
    copies = [
        pltpu.make_async_copy(src, dst, sems.at[i]) for i, (src, dst) in enumerate(moves)
    ]
    for copy in copies:
        copy.start()
    copies[0].wait()
    copies[1].wait()
    x = x_ref[...].astype(F32)
    scale = lax.rsqrt(jnp.mean(x * x, axis=-1, keepdims=True) + EPS)
    y = (x * scale * g_ref[...]).astype(BF)
    width = o_ref.shape[2]
    for b in range(o_ref.shape[0]):
        o_ref[ids[0] ^ b] = y[:, b * width:(b + 1) * width]
    copies[2].wait()
    copies[3].wait()


def first(ids, mine, gain, weight):
    far = pl.BlockSpec(memory_space=pltpu.HBM)
    half = (weight.shape[0] // 2, weight.shape[1])
    rel = (8, mine.shape[0], mine.shape[1] // 8)
    big = [pltpu.with_memory_space_constraint(a, pltpu.HBM) for a in (mine, gain, weight)]
    return pl.pallas_call(
        first_kernel,
        out_shape=[pltpu.VMEM(s, BF) for s in (rel, half, half)],
        in_specs=[SM, far, far, far],
        out_specs=[VM] * 3,
        scratch_shapes=[
            pltpu.VMEM(mine.shape, BF),
            pltpu.VMEM(gain.shape, F32),
            pltpu.SemaphoreType.DMA((4,)),
        ],
        compiler_params=pltpu.CompilerParams(vmem_limit_bytes=8 << 20),
    )(ids, *big)


def qkv_kernel(src, wa, wb, va, vb, *outs):
    half = wa.shape[0]
    for d, o_ref in enumerate(outs):
        acc = None
        for h, pair in enumerate(((wa, wb), (va, vb))):
            rows = src[:, 2 * d + h].reshape(-1, 2 * half)
            for i, w in enumerate(pair):
                part = jnp.dot(
                    rows[:, i * half:(i + 1) * half], w[...], preferred_element_type=F32
                )
                acc = part if acc is None else acc + part
        o_ref[...] = acc.astype(o_ref.dtype)


def place(row, section, step):
    group = row // step
    half = group // 8
    return (section ^ (2 * (group - 8 * half) + half)) * step + (row - group * step)


def attn_kernel(ids, a0, a1, a2, b0, b1, b2, *rest):
    wo = rest[:8]
    give, left = rest[8:10]
    packed = rest[10]
    mixed = rest[11]
    length, width = packed.shape
    half = length // 2
    for at, trio in ((0, (a0, a1, a2)), (half, (b0, b1, b2))):
        part = trio[0][...] + trio[1][...].astype(F32) + trio[2][...].astype(F32)
        packed[at:at + half, :] = part.astype(BF)
    section = ids[1]
    valid = ids[2]
    rows = place(lax.broadcasted_iota(jnp.int32, (length, 1), 0), section, 16)
    cols = place(lax.broadcasted_iota(jnp.int32, (1, length), 1), section, 16)
    allowed = (cols <= rows) & (cols < valid)
    for h in range(width // (3 * HEAD)):
        base = h * 3 * HEAD
        q = packed[:, base:base + HEAD]
        k = packed[:, base + HEAD:base + 2 * HEAD]
        v = packed[:, base + 2 * HEAD:base + 3 * HEAD]
        s = lax.dot_general(q, k, (((1,), (1,)), ((), ())), preferred_element_type=F32)
        s = jnp.where(allowed, s * (1.0 / math.sqrt(HEAD)), NEG)
        top = jnp.max(s, axis=-1, keepdims=True)
        e = jnp.where(allowed, jnp.exp(s - top), 0.0)
        p = (e / jnp.sum(e, axis=-1, keepdims=True)).astype(BF)
        mixed[:, h * HEAD:(h + 1) * HEAD] = jnp.dot(
            p, v, preferred_element_type=F32
        ).astype(BF)
    left[...] = mixed[:half, :]
    spread(mixed[half:, :], wo, give)


def spread(rows, wo, o_ref):
    width = wo[0].shape[1]
    for e in range(8):
        acc = jnp.dot(rows, wo[e][...], preferred_element_type=F32)
        o_ref[:, e * width:(e + 1) * width] = acc.astype(BF)


def keep_kernel(left, *rest):
    spread(left[...], rest[:8], rest[8])


def pair_kernel(picks, a_ref, b_ref, *outs):
    for j, o_ref in zip(picks, outs):
        rows = o_ref.shape[0]
        part = a_ref[j * rows:(j + 1) * rows, :].astype(F32) + b_ref[
            j * rows:(j + 1) * rows, :
        ].astype(F32)
        o_ref[...] = part.astype(o_ref.dtype)


def hidden_kernel(ids, frames, gain, *rest):
    pieces = rest[:5]
    o_ref = rest[5]
    acc = rest[6]
    width = frames.shape[1] // 8
    for e in range(8):
        cut = slice(e * width, (e + 1) * width)
        part = pieces[0][:, cut].astype(F32)
        for piece in pieces[1:]:
            part = part + piece[:, cut].astype(F32)
        acc[ids[0] ^ e] = part
    total = jnp.zeros((frames.shape[0], 1), F32)
    for b in range(8):
        cut = slice(b * width, (b + 1) * width)
        hid = frames[:, cut].astype(F32) + acc[b]
        acc[b] = hid
        total = total + jnp.sum(hid * hid, axis=-1, keepdims=True)
    scale = lax.rsqrt(total / frames.shape[1] + EPS)
    for b in range(8):
        cut = slice(b * width, (b + 1) * width)
        o_ref[:, cut] = (acc[b] * scale * gain[:, cut]).astype(BF)


def lift_kernel(row, src, din, emb, gain, wqkv, *outs):
    x = src[...].reshape(-1, src.shape[2])
    near = emb[row:row + 8].reshape(x.shape[0], -1).astype(F32)
    lifted = jnp.dot(x, din[...], preferred_element_type=F32) + near
    scale = lax.rsqrt(jnp.mean(lifted * lifted, axis=-1, keepdims=True) + EPS)
    dn = (lifted * scale * gain[...]).astype(BF)
    step = 1024
    for s in range(wqkv.shape[1] // step):
        cut = slice(s * step, (s + 1) * step)
        y = jnp.dot(dn, wqkv[:, cut], preferred_element_type=F32).astype(BF)
        for e in range(8):
            if len(outs) == 8:
                outs[e][:, cut] = y[e * 16:(e + 1) * 16]
            else:
                outs[0][e, :, cut] = y[e * 16:(e + 1) * 16]


def load_kernel(src, dst, sem):
    copy = pltpu.make_async_copy(src, dst, sem)
    copy.start()
    copy.wait()


def load(value):
    return pl.pallas_call(
        load_kernel,
        out_shape=pltpu.VMEM(value.shape, value.dtype),
        in_specs=[pl.BlockSpec(memory_space=pltpu.HBM)],
        out_specs=VM,
        scratch_shapes=[pltpu.SemaphoreType.DMA],
        compiler_params=pltpu.CompilerParams(vmem_limit_bytes=1 << 20),
    )(pltpu.with_memory_space_constraint(value, pltpu.HBM))


def fetch_kernel(ids, picks, dqkv, table, dqkv_o, rows_o, near, sems):
    moves = ((table, near), (dqkv, dqkv_o))
    copies = [
        pltpu.make_async_copy(src, dst, sems.at[i]) for i, (src, dst) in enumerate(moves)
    ]
    for copy in copies:
        copy.start()
    count = near.shape[0]
    entry = lax.broadcasted_iota(jnp.int32, (count, picks.shape[1]), 0)
    hot = jnp.where(entry == picks[...], 1.0, 0.0).astype(BF)
    copies[0].wait()
    rows = lax.dot_general(
        hot, near[...], (((0,), (0,)), ((), ())), preferred_element_type=F32
    ).astype(BF)
    step = rows_o.shape[1]
    for b in range(rows_o.shape[0]):
        flip = ids[1] ^ b
        rows_o[8 * (flip % 2) + flip // 2] = rows[b * step:(b + 1) * step]
    copies[1].wait()


def fetch(ids, picks, dqkv, table):
    far = pl.BlockSpec(memory_space=pltpu.HBM)
    shapes = [dqkv.shape, (16, picks.shape[1] // 16, table.shape[1])]
    big = [pltpu.with_memory_space_constraint(a, pltpu.HBM) for a in (dqkv, table)]
    return pl.pallas_call(
        fetch_kernel,
        out_shape=[pltpu.VMEM(s, BF) for s in shapes],
        in_specs=[SM, VM, far, far],
        out_specs=[VM] * 2,
        scratch_shapes=[pltpu.VMEM(table.shape, BF), pltpu.SemaphoreType.DMA((2,))],
        compiler_params=pltpu.CompilerParams(vmem_limit_bytes=14 << 20),
    )(ids, pltpu.with_memory_space_constraint(picks, pltpu.VMEM), *big)


def depth_kernel(ids, low, high, *rest):
    o_ref, z = rest[11:13]
    z[0:16, :] = low[...]
    z[128:144, :] = high[...]
    for i in range(3):
        at = (i + 1) * 16
        z[at:at + 16, :] = rest[i][0]
        z[128 + at:144 + at, :] = rest[i][1]
    for i in range(4):
        at = (i + 4) * 16
        z[at:at + 16, :] = rest[3 + i][...]
        z[128 + at:144 + at, :] = rest[7 + i][...]
    section = ids[1]
    rows = lax.broadcasted_iota(jnp.int32, (256, 1), 0)
    cols = lax.broadcasted_iota(jnp.int32, (1, 256), 1)
    rpos = place(rows, section, 16) // 16
    cpos = place(cols, section, 16) // 16
    keep = (cpos <= rpos) & (rows % 16 == cols % 16)
    bias = jnp.where(keep, 0.0, NEG)
    first = lax.broadcasted_iota(jnp.int32, (256, 2 * DHEAD), 1) < DHEAD
    inner = z.shape[1] // 3
    for pair in range(inner // (2 * DHEAD)):
        base = pair * 2 * DHEAD
        q = z[:, base:base + 2 * DHEAD]
        k = z[:, inner + base:inner + base + 2 * DHEAD]
        v = z[:, 2 * inner + base:2 * inner + base + 2 * DHEAD]
        got = []
        for side in range(2):
            mask = first if side == 0 else jnp.logical_not(first)
            qs = jnp.where(mask, q, jnp.zeros_like(q))
            s = lax.dot_general(
                qs, k, (((1,), (1,)), ((), ())), preferred_element_type=F32
            )
            s = s * (1.0 / math.sqrt(DHEAD)) + bias
            top = jnp.max(s, axis=-1, keepdims=True)
            e = jnp.exp(s - top)
            total = jnp.sum(e, axis=-1, keepdims=True)
            o = jnp.dot(e.astype(BF), v, preferred_element_type=F32)
            got.append(o / total)
        res = jnp.where(first, got[0], got[1]).astype(BF)
        for m in range(16):
            to = section ^ (2 * (m % 8) + m // 8)
            o_ref[to, :, base:base + 2 * DHEAD] = res[m * 16:(m + 1) * 16]


def add_kernel(*refs):
    part = refs[0][...].astype(F32)
    for ref in refs[1:-1]:
        part = part + ref[...].astype(F32)
    refs[-1][...] = part.astype(BF)


def add(*values):
    return call(add_kernel, [(values[0].shape, BF)], n_in=len(values), limit=2)(*values)[0]


def gather(value, across=False):
    def cb(v, flip):
        return swap(v, "cb", 16, flip)

    y = cb(value, 8)
    x3 = cb(value, 6)
    x1 = cb(value, 2)
    x2 = cb(value, 4)
    y3 = cb(y, 6)
    y1 = cb(y, 2)
    y2 = cb(y, 4) if across else cb(x2, 8)
    return [value, x1, x2, x3, y, y1, y2, y3]


def work(frames_in, valid_len, tokens, t_gain, w_qkv, w_out, h_gain, d_in, d_embed, d_gain, d_qkv):
    model = frames_in.shape[2]
    mine = frames_in[0]
    f = lax.axis_index("fsdp").astype(jnp.int32)
    c = lax.axis_index("cb").astype(jnp.int32)
    ids = jnp.stack([f, c, valid_len[0]])
    fs = lambda v, flip: swap(v, "fsdp", 8, flip)
    cb = lambda v, flip: swap(v, "cb", 16, flip)
    block = model // 8

    rel, wa, wb = first(ids, mine, t_gain[None], w_qkv)
    near = fs(w_out, 1)
    va = fs(wa, 1)
    vb = fs(wb, 1)
    local = [rel[0:2]] + [fs(rel[2 * d:2 * d + 2], 2 * d) for d in (1, 2, 3)]
    local = jnp.concatenate(local, axis=0)
    wo_even = [w_out] + [fs(w_out, 2 * d) for d in (1, 2, 3)]
    odd1, odd3 = fs(near, 2), fs(near, 6)
    odd2 = fs(wo_even[2], 1)
    wo_odd = [near, odd1, odd2, odd3]
    wo = [w for pair in zip(wo_even, wo_odd) for w in pair]
    even = jnp.stack(gather(local, True))
    odd = cb(even, 1)
    cols = w_qkv.shape[1]

    def project(src, kinds):
        return call(qkv_kernel, [((128, cols), k) for k in kinds], n_in=5)(
            src, wa, wb, va, vb
        )

    a0, a1, a2, a3 = project(even, (F32, BF, BF, F32))
    relay_a = fs(a2, 2)
    plain_a = fs(a1, 2)
    b0, b1, b2, b3 = project(odd, (F32, F32, BF, BF))
    relay_b = fs(b2, 6)
    plain_b = fs(b3, 6)
    sum_a = fs(add(a3, relay_a), 6)
    sum_b = fs(add(b1, relay_b), 2)
    give, left = call(
        attn_kernel,
        [((128, model), BF), ((128, w_out.shape[0]), BF)],
        scratch=[pltpu.VMEM((256, cols), BF), pltpu.VMEM((256, w_out.shape[0]), BF)],
        smem=1,
        n_in=15,
    )(ids, a0, plain_a, sum_a, b0, plain_b, sum_b, *wo)
    taken = cb(give, 1)
    keep = call(keep_kernel, [((128, model), BF)], n_in=9)(left, *wo)[0]
    blocks = {}
    for picks in ((6, 5, 7), (1, 3, 2, 4, 0)):
        kinds = [((16, model), BF if e else F32) for e in picks]
        run = call(functools.partial(pair_kernel, picks), kinds, n_in=2)
        blocks.update(zip(picks, run(keep, taken)))
    far3 = cb(blocks[7], 6)
    far1 = cb(blocks[5], 2)
    far2 = cb(blocks[6], 8)
    near3 = cb(blocks[3], 6)
    near1 = cb(blocks[1], 2)
    side = add(blocks[4], far1, far3)
    deep = add(blocks[2], far2)
    last2 = cb(deep, 4)
    last1 = cb(side, 8)
    pieces = [blocks[0], near1, near3, last1, last2]
    hn = call(
        hidden_kernel,
        [((16, model), BF)],
        scratch=[pltpu.VMEM((8, 16, block), F32)],
        smem=1,
        n_in=8,
    )(ids, mine, h_gain[None], *pieces)[0]
    even = jnp.stack(gather(hn))
    odd = cb(even, 1)

    din = load(d_in[0])
    dqkv, emb = fetch(ids, tokens[0], d_qkv[0], d_embed[0])
    inner = d_in.shape[2]

    def lift(src, row, outs):
        return call(functools.partial(lift_kernel, row), outs, n_in=5, limit=12)(
            src, din, emb, d_gain, dqkv
        )

    low = lift(even, 0, [((16, 3 * inner), BF)] * 8)
    high = lift(odd, 8, [((8, 16, 3 * inner), BF)])[0]
    high = cb(high, 1)
    sent = {}
    for kind, e in SENDS:
        piece = {"l": low[e], "h": high[e]}.get(kind)
        if piece is None:
            piece = jnp.stack([low[e], high[e]])
        sent[kind, e] = cb(piece, 2 * e)
    both = [sent["b", e] for e in (1, 2, 3)]
    got = [sent["l", e] for e in (4, 5, 6, 7)]
    deep = [sent["h", e] for e in (4, 5, 6, 7)]
    outs = call(
        depth_kernel,
        [((16, 16, inner), BF)],
        scratch=[pltpu.VMEM((256, 3 * inner), BF)],
        smem=1,
        n_in=14,
    )(ids, low[0], high[0], *both, *got, *deep)[0]
    out = lax.all_to_all(outs, "cb", 0, 0, tiled=True)
    return out.reshape(1, 1, 256, inner)


def solution(mesh):
    placed = (
        P("fsdp", "cb", None),
        P("fsdp"),
        P("fsdp", "cb", None),
        P(),
        P("fsdp", "cb"),
        P("cb", "fsdp"),
        P(),
        P("cb", None, None),
        P("cb", None, None),
        P("cb", None),
        P("cb", None, None),
    )
    return jax.shard_map(
        work, mesh=mesh, in_specs=placed, out_specs=P("fsdp", "cb", None, None), check_vma=False
    )
```
